512 devices in a mesh: attn: 8 (over z_lo), expert: 8 (over y, core), hidden: 4 (over x), pair: 2 (over z_hi).
Axes of the slice: x: 4, y: 4, z: 16 (z_hi: 2, z_lo: 8; z = z_hi * 8 + z_lo), core: 2. Of those that a mesh axis runs over, the one named last changes fastest.
Arguments:
- queries: bfloat16 [16, 128, 4096], P(('expert', 'pair'), None, ('attn', 'hidden')), may hold values from -5 to 5
- keys: bfloat16 [16, 128, 1024], P(('expert', 'pair'), None, 'attn'), may hold values from -5 to 5
- values: bfloat16 [16, 128, 1024], P(('expert', 'pair'), None, 'attn'), may hold values from -6 to 6
- out_weight: bfloat16 [4096, 4096], P(('attn', 'hidden')), may hold values from -0.09375 to 0.09375
- residual: bfloat16 [16, 128, 4096], P(('expert', 'pair'), ('attn', 'hidden')), may hold values from -4 to 4
- norm_gain: float32 [4096], replicated, may hold values from 0.1 to 1.9
- route_logits: float32 [16, 128, 2], P(('expert', 'pair'), ('attn', 'hidden')), may hold values from -6 to 6
- expert_ids: int32 [16, 128, 2], P(('expert', 'pair'), ('attn', 'hidden')), may hold values from 0 to 7, all different within a row; in each aligned block of 4 rows (0 to 3, 4 to 7, ..., all dimensions but the last counted through in order) at most 2 rows name the same one
- doc_lengths: int32 [16, 2], P(('expert', 'pair')), may hold values from 32 to 96, as said below
- gate_up_weight: bfloat16 [8, 2, 4096, 8192], P('expert', None, None, ('attn', 'hidden', 'pair')), may hold values from -0.09375 to 0.09375
- down_weight: bfloat16 [8, 8192, 4096], P('expert', 'attn', ('hidden', 'pair')), may hold values from -0.0625 to 0.0625
Outputs:
- layer_out: bfloat16 [16, 128, 4096], P(('expert', 'pair'), ('attn', 'hidden'))
The draws below stay inside these ranges and needn't reach their ends.
Inputs may be any that keep to these rules, and one draw needn't show every extreme that they name: `expert_ids`: A token names two different experts; in every aligned block of 4 tokens (all leading dimensions taken together, in order) no expert is named by more than 2 tokens, and in some block one expert is named by exactly 2 tokens. `doc_lengths`: each group has one document of 96 tokens and one of 32 tokens, in either order.
All inputs are finite; a program needn't handle non-finite values.
Results may differ from the reference program's by a relative error of at most 0.022.
Values may be sent and summed in bfloat16 or wider, within the bound.
No kernel may reach another device: no remote copies, remote signals or barrier semaphores. Data moves between devices by JAX's collectives and lax.ppermute only.
A program may use at most 64 MiB of HBM per device.

```python
import math
import jax
import jax.numpy as jnp
import numpy as np
from jax import lax

D = 4096
HD = 128
FF = 8192
TOK_G = 128
H = 32
KVH = 8
EXPERTS = 8
GROUPS = 16
TOK_OWN = 4
CAP = 2
SLOTS = 1024
MOST_LEN = 96


def draw_queries(key, part):
    base = jax.random.normal(jax.random.fold_in(key, 11), (GROUPS, TOK_G, H * HD), dtype=jnp.float32)
    base = jnp.clip(base, -5.0, 5.0)
    return base.astype(jnp.bfloat16)


def draw_keys(key, part):
    base = jax.random.normal(jax.random.fold_in(key, 13), (GROUPS, TOK_G, KVH * HD), dtype=jnp.float32)
    base = jnp.clip(base, -5.0, 5.0)
    return base.astype(jnp.bfloat16)


def draw_doc_lengths(key, part):
    order = jax.random.randint(jax.random.fold_in(key, 29), (GROUPS,), 0, 2, dtype=jnp.int32)
    longest = jnp.full((GROUPS,), MOST_LEN, dtype=jnp.int32)
    shortest = jnp.full((GROUPS,), TOK_G - MOST_LEN, dtype=jnp.int32)
    first = jnp.where(order > 0, longest, shortest)
    second = jnp.where(order > 0, shortest, longest)
    return jnp.stack([first, second], axis=1).astype(jnp.int32)


def levels(stream_key, shape, shards, smallest, largest):
    gain, own = 1.0, jax.random.fold_in(stream_key, 6)
    for position, shards_of in shards:
        heights = jnp.exp(jax.random.uniform(jax.random.fold_in(own, position), (shards_of,), jnp.float32, smallest / len(shards), largest / len(shards)))
        gain = gain * jnp.repeat(heights, shape[position] // shards_of).reshape([-1 if axis == position else 1 for axis in range(len(shape))])
    return gain


def routed_block(stream_key, own, number, rows, amount, top, reach, lean):
    sequence = jax.random.permutation(stream_key, amount)
    packed, ordinary = load_shares(amount, rows * top, reach, lean, True), load_shares(amount, rows * top, reach, lean, False)
    places = jnp.arange(amount)

    def named(sizes, rotation):
        used = int((sizes > 0).sum())
        fixed = max(1, used // 4)
        moved = fixed + (places - fixed + rotation * (used - fixed)) % max(1, amount - fixed)
        return jnp.zeros((amount,), jnp.int32).at[sequence[jnp.where(places < fixed, places, moved)]].set(jnp.asarray(sizes, jnp.int32))

    sizes = jnp.where(number % 4 == 0, named(packed, number // 4), named(ordinary, number - number // 4 - 1))
    mixed = jax.random.permutation(jax.random.fold_in(own, 3), amount)
    giver, sink = mixed[0:amount // 2 * 2:2], mixed[1:amount // 2 * 2:2]
    room = jnp.minimum(sizes[giver] - 1, reach - sizes[sink]) // 2
    room = jnp.where((giver == sequence[0]) | (sink == sequence[0]) | (sizes[sink] == 0), 0, jnp.maximum(room, 0))
    moved = jax.random.randint(jax.random.fold_in(own, 4), (amount // 2,), 0, 1 << 20) % (room + 1)
    sizes = sizes.at[giver].add(-moved).at[sink].add(moved)
    labels = jnp.searchsorted(jnp.cumsum(sizes), jnp.arange(rows * top), side="right").astype(jnp.int32)
    grid = labels.reshape(top, rows).T
    grid = grid[jax.random.permutation(jax.random.fold_in(own, 1), rows)]
    rotation = jax.random.randint(jax.random.fold_in(own, 2), (rows, 1), 0, top)
    return jnp.take_along_axis(grid, (jnp.arange(top)[None, :] + rotation) % top, axis=1)


def load_shares(amount, total, bound, slope, full):
    portions = [(1 << 20) // math.isqrt(rank ** slope) + 1 for rank in range(1, amount + 1)]
    largest = bound if full else min(bound, max(-(-total // amount), total * portions[0] // sum(portions)))
    least = 1 if total - largest >= amount - 1 else 0
    counts, surplus = [largest] + [least] * (amount - 1), total - largest - least * (amount - 1)
    while surplus > 0:
        movable = [i for i in range(1, amount) if counts[i] < largest] or [i for i in range(1, amount) if counts[i] < bound]
        mass, remaining = sum([portions[i] for i in movable]), surplus
        for i in movable:
            extra = min(bound - counts[i], max(1, remaining * portions[i] // mass), surplus)
            counts[i] = counts[i] + extra
            surplus = surplus - extra
    return np.array(counts)


def gaussian(own_key, dims, deviation, bound, pieces=(), kind=jnp.bfloat16):
    entries = jax.random.normal(own_key, dims, jnp.float32) * deviation
    if len(pieces) > 0:
        entries = levels(own_key, dims, pieces, -0.22, 0.18) * entries
    return jnp.clip(entries, min=-bound, max=bound).astype(kind)


def setup_inputs(seed: int = 0) -> dict:
    key_list = jax.random.split(jax.random.key(seed), 12)
    queries = draw_queries(jax.random.fold_in(key_list[11], 71), 0)
    keys = draw_keys(jax.random.fold_in(key_list[11], 71), 0)
    values = gaussian(key_list[2], (GROUPS, TOK_G, KVH * HD), 1.0, 6.0, ((0, 16), (2, 8)))
    out_weight = gaussian(key_list[3], (H * HD, D), (H * HD) ** -0.5, 0.09375, ((0, 32),))
    residual = gaussian(key_list[4], (GROUPS, TOK_G, D), 0.5, 4.0, ((0, 16), (1, 32)))
    norm_gain = jnp.clip(1.0 + 0.18 * jax.random.normal(key_list[5], (D,), jnp.float32), 0.1, 1.9)
    route_logits = gaussian(key_list[6], (GROUPS, TOK_G, 2), 1.5, 6.0, ((0, 16), (1, 32)), jnp.float32)
    expert_ids_keys = jax.random.split(jax.random.fold_in(key_list[7], 1), GROUPS * TOK_G // TOK_OWN)
    expert_ids_turns = jax.random.permutation(jax.random.fold_in(key_list[7], 3), GROUPS * TOK_G // TOK_OWN)
    expert_ids = jax.vmap(lambda own, number: routed_block(jax.random.fold_in(key_list[7], 2), own, number, TOK_OWN, EXPERTS, 2, CAP, 2))(expert_ids_keys, expert_ids_turns).reshape((GROUPS, TOK_G, 2))
    doc_lengths = draw_doc_lengths(jax.random.fold_in(key_list[11], 71), 0)
    gate_up_weight = gaussian(key_list[9], (EXPERTS, 2, D, FF), D ** -0.5, 0.09375, ((0, 8), (3, 64)))
    down_weight = gaussian(key_list[10], (EXPERTS, FF, D), FF ** -0.5, 0.0625, ((0, 8), (1, 8), (2, 8)))
    return dict(queries=queries, keys=keys, values=values, out_weight=out_weight, residual=residual, norm_gain=norm_gain, route_logits=route_logits, expert_ids=expert_ids, doc_lengths=doc_lengths, gate_up_weight=gate_up_weight, down_weight=down_weight)


epsilon = 1e-05

def document_mask(lengths):
    doc_ends = jnp.cumsum(lengths)
    positions = jnp.arange(TOK_G, dtype=jnp.int32)
    document = lax.optimization_barrier(jnp.sum((positions[:, None] >= doc_ends[None, :]).astype(jnp.int32), axis=1))
    same_doc = document[:, None] == document[None, :]
    return (same_doc & (positions[None, :] <= positions[:, None])).astype(jnp.int32)

def attend_head(query_rows, key_rows, value_rows, allowed):
    scores = jnp.dot(query_rows, key_rows.T, preferred_element_type=jnp.float32) * HD ** (-0.5)
    scores = jnp.where(allowed > 0, scores, -1e+30)
    row_top = lax.optimization_barrier(jnp.max(scores, axis=1, keepdims=True))
    weights = jnp.exp(scores - row_top)
    probabilities = (weights / lax.optimization_barrier(jnp.sum(weights, axis=1, keepdims=True))).astype(jnp.bfloat16)
    return jnp.dot(probabilities, value_rows, preferred_element_type=jnp.float32).astype(jnp.bfloat16)

def reference(queries, keys, values, out_weight, residual, norm_gain, route_logits, expert_ids, doc_lengths, gate_up_weight, down_weight):

    def group_forward(inputs):
        query_group, key_group, value_group, resid_group, lengths = inputs
        allowed = document_mask(lengths)
        share = H // KVH
        query_heads = query_group.reshape(TOK_G, H, HD).transpose(1, 0, 2)
        key_heads = jnp.repeat(key_group.reshape(TOK_G, KVH, HD).transpose(1, 0, 2), share, axis=0)
        value_heads = jnp.repeat(value_group.reshape(TOK_G, KVH, HD).transpose(1, 0, 2), share, axis=0)
        heads_out = jax.vmap(attend_head, in_axes=(0, 0, 0, None))(query_heads, key_heads, value_heads, allowed)
        joined = heads_out.transpose(1, 0, 2).reshape(TOK_G, H * HD)
        attended = resid_group.astype(jnp.float32) + jnp.dot(joined, out_weight, preferred_element_type=jnp.float32)
        scale = lax.rsqrt(lax.optimization_barrier(jnp.mean(attended * attended, axis=1, keepdims=True)) + epsilon)
        normed = (attended * scale * norm_gain).astype(jnp.bfloat16)
        return (attended, normed)
    attended, normed = lax.map(group_forward, (queries, keys, values, residual, doc_lengths))
    owners = GROUPS * TOK_G // TOK_OWN
    row_total = 2 * TOK_OWN
    chosen = expert_ids.reshape(owners, row_total)
    row_ids = jnp.arange(row_total, dtype=jnp.int32)
    earlier = row_ids[None, :] < row_ids[:, None]
    same_expert = chosen[:, :, None] == chosen[:, None, :]
    ranking = lax.optimization_barrier(jnp.sum((same_expert & earlier[None]).astype(jnp.int32), axis=2))
    owner_ids = jnp.arange(owners, dtype=jnp.int32)
    slot_of_row = (chosen * SLOTS + owner_ids[:, None] * CAP + ranking).reshape(-1)
    token_of_row = (owner_ids[:, None] * TOK_OWN + row_ids[None, :] // 2).reshape(-1)
    slot_token = jnp.zeros((EXPERTS * SLOTS,), jnp.int32).at[slot_of_row].set(token_of_row)
    slot_filled = jnp.zeros((EXPERTS * SLOTS,), jnp.int32).at[slot_of_row].set(1)
    flat_normed = normed.reshape(GROUPS * TOK_G, D)
    picked = jnp.take(flat_normed, slot_token, axis=0)
    picked = jnp.where(slot_filled[:, None] > 0, picked, jnp.zeros_like(picked))
    expert_rows = picked.reshape(EXPERTS, SLOTS, D)

    def expert_forward(inputs):
        rows, gate_up, down = inputs
        gate = jnp.dot(rows, gate_up[0], preferred_element_type=jnp.float32)
        upward = jnp.dot(rows, gate_up[1], preferred_element_type=jnp.float32)
        activated = (jax.nn.silu(gate) * upward).astype(jnp.bfloat16)
        return jnp.dot(activated, down, preferred_element_type=jnp.float32).astype(jnp.bfloat16)
    expert_out = lax.map(expert_forward, (expert_rows, gate_up_weight, down_weight)).reshape(EXPERTS * SLOTS, D)
    row_out = jnp.take(expert_out, slot_of_row, axis=0).reshape(GROUPS, TOK_G, 2, D).astype(jnp.float32)
    first_share = jax.nn.sigmoid(route_logits[..., 0] - route_logits[..., 1])
    layer_out = attended + first_share[..., None] * row_out[:, :, 0] + (1.0 - first_share)[..., None] * row_out[:, :, 1]
    return layer_out.astype(jnp.bfloat16)
```

```python
import jax
import jax.numpy as jnp
from jax import lax
from jax.sharding import Mesh
from jax.sharding import PartitionSpec as P

D = 4096
HD = 128
EPSILON = 1e-05
BF16 = jnp.bfloat16
F32 = jnp.float32


ATTN = ("ab", "aa")
Z_AXES = ("ab", "aa", "pair")
ROUTE = ("y", "core", "pair", "ab", "hidden")


def z_shift(step):
    def place(z):
        return ((z % 8) // 4) * 8 + (z % 4) * 2 + z // 8

    return [(place(z), place((z + step) % 16)) for z in range(16)]


def exchange(value, axes):
    return lax.all_to_all(value, axes, 0, 0, tiled=True)


def attention(queries, keys, values, doc_lengths):
    tok_group = queries.shape[0]
    doc_ends = jnp.cumsum(doc_lengths)
    positions = jnp.arange(tok_group, dtype=jnp.int32)
    document = jnp.sum((positions[:, None] >= doc_ends[None, :]).astype(jnp.int32), axis=1)
    allowed = (document[:, None] == document[None, :]) & (positions[None, :] <= positions[:, None])
    scores = jnp.dot(queries, keys.T, preferred_element_type=F32) * HD ** (-0.5)
    scores = jnp.where(allowed, scores, -1e30)
    row_top = jnp.max(scores, axis=1, keepdims=True)
    weights = jnp.exp(scores - row_top)
    probabilities = (weights / jnp.sum(weights, axis=1, keepdims=True)).astype(BF16)
    return jnp.dot(probabilities, values, preferred_element_type=F32).astype(BF16)


def slot_selector(chosen, experts, capacity):
    rows = chosen.shape[0]
    row_ids = jnp.arange(rows, dtype=jnp.int32)
    earlier = row_ids[None, :] < row_ids[:, None]
    same = chosen[:, None] == chosen[None, :]
    ranking = jnp.sum((same & earlier).astype(jnp.int32), axis=-1)
    slots = jnp.arange(experts * capacity, dtype=jnp.int32)
    return (chosen[None, :] == (slots // capacity)[:, None]) & (
        ranking[None, :] == (slots % capacity)[:, None]
    )


def body(
    queries,
    keys,
    values,
    out_weight,
    residual,
    norm_gain,
    route_logits,
    expert_ids,
    doc_lengths,
    gate_up_weight,
    down_weight,
):
    xs = lax.axis_size("hidden")
    zl = lax.axis_size(ATTN)
    pairs = lax.axis_size("pair")
    experts = lax.axis_size(("y", "core"))
    capacity = 2
    chunk = D // xs
    z_hi = lax.axis_index("pair")

    gate_up = gate_up_weight[0].reshape(2, xs, chunk, -1).transpose(1, 0, 2, 3)
    gate_up = exchange(gate_up, "hidden")
    unit = gate_up.shape[-1]
    gate_up = gate_up.transpose(2, 1, 0, 3).reshape(chunk, 2 * xs * unit)
    down = down_weight[0].reshape(xs, pairs, unit, -1)
    width = down.shape[-1]
    kept = lax.dynamic_index_in_dim(down, z_hi, 1, keepdims=False).reshape(xs * unit, width)
    sent = lax.dynamic_index_in_dim(down, 1 - z_hi, 1, keepdims=False).reshape(xs * unit, width)
    other = lax.ppermute(sent, "pair", [(0, 1), (1, 0)])
    down = jnp.concatenate(
        [jnp.where(z_hi == 0, kept, other), jnp.where(z_hi == 0, other, kept)], axis=1
    )

    heads_out = attention(queries[0], keys[0], values[0], doc_lengths[0])
    tok_group = heads_out.shape[0]
    owned = tok_group // (zl * xs)
    projected = jnp.dot(heads_out, out_weight, preferred_element_type=F32).astype(BF16)
    projected = projected.reshape(zl, xs, owned, D).transpose(1, 0, 2, 3)
    projected = jnp.sum(exchange(projected, "hidden").astype(F32), axis=0).astype(BF16)
    projected = jnp.sum(exchange(projected, ATTN).astype(F32), axis=0)
    attended = residual[0].astype(F32) + projected
    scale = lax.rsqrt(jnp.mean(attended * attended, axis=1, keepdims=True) + EPSILON)
    normed = (attended * scale * norm_gain).astype(BF16)

    chosen = expert_ids[0].reshape(2 * owned)
    selector = slot_selector(chosen, experts, capacity)
    picker = selector[:, 0::2] | selector[:, 1::2]
    picked = jnp.dot(picker.astype(BF16), normed, preferred_element_type=F32).astype(BF16)
    picked = picked.reshape(experts, 1, capacity, xs, chunk).transpose(0, 1, 3, 2, 4)
    far = lax.axis_size(("pair", "ab"))
    outgoing = jnp.broadcast_to(picked, (experts, far, xs, capacity, chunk))
    rows = exchange(outgoing.reshape(-1, capacity, chunk), ROUTE).reshape(-1, chunk)
    steps = (1, -1, 2)
    window = [rows] + [lax.ppermute(rows, Z_AXES, z_shift(d)) for d in steps]

    rows = jnp.concatenate(window, axis=0)
    partial = jnp.dot(rows, gate_up, preferred_element_type=F32).astype(BF16)
    partial = partial.reshape(xs, -1, partial.shape[1])
    summed = jnp.sum(exchange(partial, "hidden").astype(F32), axis=0)
    half = xs * unit
    activated = (jax.nn.silu(summed[:, :half]) * summed[:, half:]).astype(BF16)
    activated = exchange(jnp.broadcast_to(activated, (xs, *activated.shape)), "hidden")
    activated = activated.reshape(-1, half)
    out = jnp.dot(activated, down, preferred_element_type=F32)
    blocks = out.reshape(len(window), -1, chunk)
    total = blocks[0]
    for k, d in enumerate(steps):
        back = lax.ppermute(blocks[k + 1].astype(BF16), Z_AXES, z_shift(-d))
        total = total + back.astype(F32)

    total = total.astype(BF16).reshape(-1, capacity, chunk)
    returned = exchange(total, ROUTE).reshape(experts, far, xs, capacity, chunk)
    returned = jnp.sum(returned.astype(F32), axis=1).astype(BF16)
    returned = returned.transpose(0, 2, 1, 3).reshape(experts * capacity, D)
    per_row = jnp.einsum(
        "sr,sd->rd", selector.astype(BF16), returned, preferred_element_type=F32
    ).reshape(owned, 2, D)
    logits = route_logits[0]
    first_share = jax.nn.sigmoid(logits[:, 0] - logits[:, 1])
    layer_out = (
        attended
        + first_share[:, None] * per_row[:, 0]
        + (1.0 - first_share)[:, None] * per_row[:, 1]
    )
    return layer_out.astype(BF16)[None]


def solution(mesh):
    cut = Mesh(
        mesh.devices.reshape(2, 4, 4, 2, 4, 2), ("ab", "aa", "y", "core", "hidden", "pair")
    )
    expert = ("y", "core")
    group = ("y", "core", "pair")
    owner = ("ab", "aa", "hidden")
    in_specs = (
        P(group, None, owner),
        P(group, None, ATTN),
        P(group, None, ATTN),
        P(owner, None),
        P(group, owner, None),
        P(),
        P(group, owner, None),
        P(group, owner, None),
        P(group, None),
        P(expert, None, None, ("ab", "aa", "hidden", "pair")),
        P(expert, ATTN, ("hidden", "pair")),
    )
    return jax.shard_map(
        body, mesh=cut, in_specs=in_specs, out_specs=P(group, owner, None), check_vma=False
    )
```

```python
import jax
import jax.numpy as jnp
from jax import lax
from jax.sharding import Mesh
from jax.sharding import PartitionSpec as P


D = 4096
HD = 128
EPSILON = 1e-05
BF16 = jnp.bfloat16
F32 = jnp.float32


ATTN = ("ab", "aa")
Z_AXES = ("ab", "aa", "pair")
ROUTE = ("y", "core", "pair", "ab", "hidden")


def z_shift(step):
    def place(z):
        return ((z % 8) // 4) * 8 + (z % 4) * 2 + z // 8

    return [(place(z), place((z + step) % 16)) for z in range(16)]


def exchange(value, axes):
    return lax.all_to_all(value, axes, 0, 0, tiled=True)


def attention(queries, keys, values, doc_lengths):
    tok_group = queries.shape[0]
    doc_ends = jnp.cumsum(doc_lengths)
    positions = jnp.arange(tok_group, dtype=jnp.int32)
    document = jnp.sum((positions[:, None] >= doc_ends[None, :]).astype(jnp.int32), axis=1)
    allowed = (document[:, None] == document[None, :]) & (positions[None, :] <= positions[:, None])
    scores = jnp.dot(queries, keys.T, preferred_element_type=F32) * HD ** (-0.5)
    scores = jnp.where(allowed, scores, -1e30)
    row_top = jnp.max(scores, axis=1, keepdims=True)
    weights = jnp.exp(scores - row_top)
    probabilities = (weights / jnp.sum(weights, axis=1, keepdims=True)).astype(BF16)
    return jnp.dot(probabilities, values, preferred_element_type=F32).astype(BF16)


def slot_selector(chosen, experts, capacity):
    rows = chosen.shape[0]
    row_ids = jnp.arange(rows, dtype=jnp.int32)
    earlier = row_ids[None, :] < row_ids[:, None]
    same = chosen[:, None] == chosen[None, :]
    ranking = jnp.sum((same & earlier).astype(jnp.int32), axis=-1)
    slots = jnp.arange(experts * capacity, dtype=jnp.int32)
    return (chosen[None, :] == (slots // capacity)[:, None]) & (
        ranking[None, :] == (slots % capacity)[:, None]
    )


def layer(
    queries,
    keys,
    values,
    out_weight,
    residual,
    norm_gain,
    route_logits,
    expert_ids,
    doc_lengths,
    gate_up_weight,
    down_weight,
):
    xs = lax.axis_size("hidden")
    zl = lax.axis_size(ATTN)
    pairs = lax.axis_size("pair")
    experts = lax.axis_size(("y", "core"))
    capacity = 2
    chunk = D // xs
    z_hi = lax.axis_index("pair")

    unit = gate_up_weight.shape[-1]
    down = down_weight[0].reshape(xs, pairs, unit, -1)
    width = down.shape[-1]
    kept = lax.dynamic_index_in_dim(down, z_hi, 1, keepdims=False).reshape(xs * unit, width)
    sent = lax.dynamic_index_in_dim(down, 1 - z_hi, 1, keepdims=False).reshape(xs * unit, width)
    other = lax.ppermute(sent, "pair", [(0, 1), (1, 0)])
    down = jnp.concatenate(
        [jnp.where(z_hi == 0, kept, other), jnp.where(z_hi == 0, other, kept)], axis=1
    )

    heads_out = attention(queries[0], keys[0], values[0], doc_lengths[0])
    tok_group = heads_out.shape[0]
    owned = tok_group // (zl * xs)
    projected = jnp.dot(heads_out, out_weight, preferred_element_type=F32).astype(BF16)
    projected = projected.reshape(zl, xs, owned, D).transpose(1, 0, 2, 3)
    projected = jnp.sum(exchange(projected, "hidden").astype(F32), axis=0).astype(BF16)
    gate_up = gate_up_weight[0].reshape(2, xs, chunk, unit)
    projected, gate_up = lax.optimization_barrier((projected, gate_up))
    me = lax.axis_index("hidden")
    gathered = jnp.zeros((xs, 2, chunk, unit), BF16)
    for d in range(xs):
        block = lax.dynamic_index_in_dim(gate_up, (me + d) % xs, 1, keepdims=False)
        if d > 0:
            block = lax.ppermute(block, "hidden", [(i, (i + d) % xs) for i in range(xs)])
        gathered = lax.dynamic_update_index_in_dim(gathered, block, (me - d) % xs, 0)
    projected = jnp.sum(exchange(projected, ATTN).astype(F32), axis=0)
    gate_up = gathered.transpose(2, 1, 0, 3).reshape(chunk, 2 * xs * unit)
    attended = residual[0].astype(F32) + projected
    scale = lax.rsqrt(jnp.mean(attended * attended, axis=1, keepdims=True) + EPSILON)
    normed = (attended * scale * norm_gain).astype(BF16)

    chosen = expert_ids[0].reshape(2 * owned)
    selector = slot_selector(chosen, experts, capacity)
    picker = selector[:, 0::2] | selector[:, 1::2]
    picked = jnp.dot(picker.astype(BF16), normed, preferred_element_type=F32).astype(BF16)
    picked = picked.reshape(experts, 1, capacity, xs, chunk).transpose(0, 1, 3, 2, 4)
    far = lax.axis_size(("pair", "ab"))
    outgoing = jnp.broadcast_to(picked, (experts, far, xs, capacity, chunk))
    rows = exchange(outgoing.reshape(-1, capacity, chunk), ROUTE).reshape(-1, chunk)
    steps = (1, -1, 2)
    window = [rows] + [lax.ppermute(rows, Z_AXES, z_shift(d)) for d in steps]

    rows = jnp.concatenate(window, axis=0)
    partial = jnp.dot(rows, gate_up, preferred_element_type=F32).astype(BF16)
    partial = partial.reshape(xs, -1, partial.shape[1])
    summed = jnp.sum(exchange(partial, "hidden").astype(F32), axis=0)
    half = xs * unit
    activated = (jax.nn.silu(summed[:, :half]) * summed[:, half:]).astype(BF16)
    activated = exchange(jnp.broadcast_to(activated, (xs, *activated.shape)), "hidden")
    activated = activated.reshape(-1, half)
    out = jnp.dot(activated, down, preferred_element_type=F32)
    blocks = out.reshape(len(window), -1, chunk)
    total = blocks[0]
    for k, d in enumerate(steps):
        back = lax.ppermute(blocks[k + 1].astype(BF16), Z_AXES, z_shift(-d))
        total = total + back.astype(F32)

    total = total.astype(BF16).reshape(-1, capacity, chunk)
    returned = exchange(total, ROUTE).reshape(experts, far, xs, capacity, chunk)
    returned = jnp.sum(returned.astype(F32), axis=1).astype(BF16)
    returned = returned.transpose(0, 2, 1, 3).reshape(experts * capacity, D)
    per_row = jnp.einsum(
        "sr,sd->rd", selector.astype(BF16), returned, preferred_element_type=F32
    ).reshape(owned, 2, D)
    logits = route_logits[0]
    first_share = jax.nn.sigmoid(logits[:, 0] - logits[:, 1])
    layer_out = (
        attended
        + first_share[:, None] * per_row[:, 0]
        + (1.0 - first_share)[:, None] * per_row[:, 1]
    )
    return layer_out.astype(BF16)[None]


def solution(mesh):
    cut = Mesh(
        mesh.devices.reshape(2, 4, 4, 2, 4, 2), ("ab", "aa", "y", "core", "hidden", "pair")
    )
    expert = ("y", "core")
    group = ("y", "core", "pair")
    owner = ("ab", "aa", "hidden")
    in_specs = (
        P(group, None, owner),
        P(group, None, ATTN),
        P(group, None, ATTN),
        P(owner, None),
        P(group, owner, None),
        P(),
        P(group, owner, None),
        P(group, owner, None),
        P(group, None),
        P(expert, None, None, ("ab", "aa", "hidden", "pair")),
        P(expert, ATTN, ("hidden", "pair")),
    )
    return jax.shard_map(
        layer, mesh=cut, in_specs=in_specs, out_specs=P(group, owner, None), check_vma=False
    )
```

```python
import jax
import jax.numpy as jnp
from jax import lax
from jax.sharding import Mesh
from jax.sharding import PartitionSpec as P


D = 4096
HD = 128
EPSILON = 1e-05
BF16 = jnp.bfloat16
F32 = jnp.float32


ATTN = ("ab", "aa")
Z_AXES = ("ab", "aa", "core", "pair")
ROUTE = ("y", "core", "pair", "ab", "hidden")


def z_shift(steps):
    def place(z, core):
        return (((z % 8) * 2) + core) * 2 + z // 8

    return [
        (place(z, core), place((z + steps[core]) % 16, core)) for z in range(16) for core in (0, 1)
    ]


def exchange(value, axes):
    return lax.all_to_all(value, axes, 0, 0, tiled=True)


def attention(queries, keys, values, doc_lengths):
    tok_group = queries.shape[0]
    doc_ends = jnp.cumsum(doc_lengths)
    positions = jnp.arange(tok_group, dtype=jnp.int32)
    document = jnp.sum((positions[:, None] >= doc_ends[None, :]).astype(jnp.int32), axis=1)
    allowed = (document[:, None] == document[None, :]) & (positions[None, :] <= positions[:, None])
    scores = jnp.dot(queries, keys.T, preferred_element_type=F32) * HD ** (-0.5)
    scores = jnp.where(allowed, scores, -1e30)
    row_top = jnp.max(scores, axis=1, keepdims=True)
    weights = jnp.exp(scores - row_top)
    probabilities = (weights / jnp.sum(weights, axis=1, keepdims=True)).astype(BF16)
    return jnp.dot(probabilities, values, preferred_element_type=F32).astype(BF16)


def slot_selector(chosen, experts, capacity):
    rows = chosen.shape[0]
    row_ids = jnp.arange(rows, dtype=jnp.int32)
    earlier = row_ids[None, :] < row_ids[:, None]
    same = chosen[:, None] == chosen[None, :]
    ranking = jnp.sum((same & earlier).astype(jnp.int32), axis=-1)
    slots = jnp.arange(experts * capacity, dtype=jnp.int32)
    return (chosen[None, :] == (slots // capacity)[:, None]) & (
        ranking[None, :] == (slots % capacity)[:, None]
    )


def layer(
    queries,
    keys,
    values,
    out_weight,
    residual,
    norm_gain,
    route_logits,
    expert_ids,
    doc_lengths,
    gate_up_weight,
    down_weight,
):
    xs = lax.axis_size("hidden")
    zl = lax.axis_size(ATTN)
    pairs = lax.axis_size("pair")
    experts = lax.axis_size(("y", "core"))
    capacity = 2
    chunk = D // xs
    z_hi = lax.axis_index("pair")

    unit = gate_up_weight.shape[-1]
    down = down_weight[0].reshape(xs, pairs, unit, -1)
    width = down.shape[-1]
    kept = lax.dynamic_index_in_dim(down, z_hi, 1, keepdims=False)
    sent = lax.dynamic_index_in_dim(down, 1 - z_hi, 1, keepdims=False)
    swap = [(0, 1), (1, 0)]
    other_a = lax.ppermute(sent[: xs // 2], "pair", swap)

    heads_out = attention(queries[0], keys[0], values[0], doc_lengths[0])
    tok_group = heads_out.shape[0]
    owned = tok_group // (zl * xs)
    projected = jnp.dot(heads_out, out_weight, preferred_element_type=F32).astype(BF16)
    projected = projected.reshape(zl, xs, owned, D).transpose(1, 0, 2, 3)
    projected = jnp.sum(exchange(projected, "hidden").astype(F32), axis=0).astype(BF16)
    gate_up = gate_up_weight[0].reshape(2, xs, chunk, unit)
    me = lax.axis_index("hidden")
    gathered = jnp.zeros((xs, 2, chunk, unit), BF16)
    for d in range(xs):
        block = lax.dynamic_index_in_dim(gate_up, (me + d) % xs, 1, keepdims=False)
        if d > 0:
            block = lax.ppermute(block, "hidden", [(i, (i + d) % xs) for i in range(xs)])
        gathered = lax.dynamic_update_index_in_dim(gathered, block, (me - d) % xs, 0)
    projected = jnp.sum(exchange(projected, ATTN).astype(F32), axis=0)
    gate_up = gathered.transpose(2, 1, 0, 3).reshape(chunk, 2 * xs * unit)
    attended = residual[0].astype(F32) + projected
    scale = lax.rsqrt(jnp.mean(attended * attended, axis=1, keepdims=True) + EPSILON)
    normed = (attended * scale * norm_gain).astype(BF16)

    chosen = expert_ids[0].reshape(2 * owned)
    selector = slot_selector(chosen, experts, capacity)
    picker = selector[:, 0::2] | selector[:, 1::2]
    picked = jnp.dot(picker.astype(BF16), normed, preferred_element_type=F32).astype(BF16)
    picked = picked.reshape(experts, 1, capacity, xs, chunk).transpose(0, 1, 3, 2, 4)
    far = lax.axis_size(("pair", "ab"))
    outgoing = jnp.broadcast_to(picked, (experts, far, xs, capacity, chunk))
    rows = exchange(outgoing.reshape(-1, capacity, chunk), ROUTE).reshape(-1, chunk)
    steps = ((1, 1), (-1, -1), (2, -2))
    window = [rows] + [lax.ppermute(rows, Z_AXES, z_shift(d)) for d in steps]

    rows = jnp.concatenate(window, axis=0)
    partial = jnp.dot(rows, gate_up, preferred_element_type=F32).astype(BF16)
    partial = partial.reshape(xs, -1, partial.shape[1])
    partial, sent_b = lax.optimization_barrier((partial, sent[xs // 2 :]))
    other_b = lax.ppermute(sent_b, "pair", swap)
    summed = jnp.sum(exchange(partial, "hidden").astype(F32), axis=0)
    half = xs * unit
    activated = (jax.nn.silu(summed[:, :half]) * summed[:, half:]).astype(BF16)
    activated = exchange(jnp.broadcast_to(activated, (xs, *activated.shape)), "hidden")
    activated = activated.reshape(-1, half)
    kept = kept.reshape(half, width)
    other = jnp.concatenate([other_a, other_b], axis=0).reshape(half, width)
    down = jnp.concatenate(
        [jnp.where(z_hi == 0, kept, other), jnp.where(z_hi == 0, other, kept)], axis=1
    )
    out = jnp.dot(activated, down, preferred_element_type=F32)
    blocks = out.reshape(len(window), -1, chunk)
    total = blocks[0]
    for n, d in enumerate(steps):
        back = lax.ppermute(blocks[n + 1].astype(BF16), Z_AXES, z_shift([-k for k in d]))
        total = total + back.astype(F32)

    total = total.astype(BF16).reshape(-1, capacity, chunk)
    returned = exchange(total, ROUTE).reshape(experts, far, xs, capacity, chunk)
    returned = jnp.sum(returned.astype(F32), axis=1).astype(BF16)
    returned = returned.transpose(0, 2, 1, 3).reshape(experts * capacity, D)
    per_row = jnp.einsum(
        "sr,sd->rd", selector.astype(BF16), returned, preferred_element_type=F32
    ).reshape(owned, 2, D)
    logits = route_logits[0]
    first_share = jax.nn.sigmoid(logits[:, 0] - logits[:, 1])
    layer_out = (
        attended
        + first_share[:, None] * per_row[:, 0]
        + (1.0 - first_share)[:, None] * per_row[:, 1]
    )
    return layer_out.astype(BF16)[None]


def solution(mesh):
    cut = Mesh(
        mesh.devices.reshape(2, 4, 4, 2, 4, 2), ("ab", "aa", "y", "core", "hidden", "pair")
    )
    expert = ("y", "core")
    group = ("y", "core", "pair")
    owner = ("ab", "aa", "hidden")
    in_specs = (
        P(group, None, owner),
        P(group, None, ATTN),
        P(group, None, ATTN),
        P(owner, None),
        P(group, owner, None),
        P(),
        P(group, owner, None),
        P(group, owner, None),
        P(group, None),
        P(expert, None, None, ("ab", "aa", "hidden", "pair")),
        P(expert, ATTN, ("hidden", "pair")),
    )
    return jax.shard_map(
        layer, mesh=cut, in_specs=in_specs, out_specs=P(group, owner, None), check_vma=False
    )
```

```python
import jax
import jax.numpy as jnp
from jax import lax
from jax.experimental import pallas as pl
from jax.sharding import Mesh
from jax.sharding import PartitionSpec as P


D = 4096
HD = 128
EPSILON = 1e-05
BF16 = jnp.bfloat16
F32 = jnp.float32


ATTN = ("ab", "aa")
Z_AXES = ("pair", "ab", "aa")
ROUTE = ("hidden", "y", "core")
LANES = 128


def exchange(value, axes):
    return lax.all_to_all(value, axes, 0, 0, tiled=True)


def attention(queries, keys, values, doc_lengths):
    tok_group = queries.shape[0]
    doc_ends = jnp.cumsum(doc_lengths)
    positions = jnp.arange(tok_group, dtype=jnp.int32)
    document = jnp.sum((positions[:, None] >= doc_ends[None, :]).astype(jnp.int32), axis=1)
    allowed = (document[:, None] == document[None, :]) & (positions[None, :] <= positions[:, None])
    scores = jnp.dot(queries, keys.T, preferred_element_type=F32) * HD ** (-0.5)
    scores = jnp.where(allowed, scores, -1e30)
    row_top = jnp.max(scores, axis=1, keepdims=True)
    weights = jnp.exp(scores - row_top)
    probabilities = (weights / jnp.sum(weights, axis=1, keepdims=True)).astype(BF16)
    return jnp.dot(probabilities, values, preferred_element_type=F32).astype(BF16)


def slot_numbers(chosen, place, places, capacity):
    rows = chosen.shape[0]
    row_ids = jnp.arange(rows, dtype=jnp.int32)
    earlier = row_ids[None, :] < row_ids[:, None]
    same = chosen[:, None] == chosen[None, :]
    ranking = jnp.sum((same & earlier).astype(jnp.int32), axis=-1)
    return (chosen * places + place) * capacity + ranking


def note_of(slots, share):
    high = lax.reduce_precision(share, 8, 7)
    middle = lax.reduce_precision(share - high, 8, 7)
    low = share - high - middle
    parts = jnp.stack([slots[:, 0].astype(F32), slots[:, 1].astype(F32), high, middle, low], axis=1)
    return jnp.pad(parts, ((0, 0), (0, LANES - 5))).astype(BF16)


def pick_kernel(tokens_ref, note_ref, out_ref):
    note = note_ref[...].astype(F32)
    slots = lax.broadcasted_iota(jnp.int32, (note.shape[0], out_ref.shape[1]), 1).astype(F32)
    taken = (slots == note[:, 0:1]) | (slots == note[:, 1:2])
    out_ref[0] = lax.dot_general(
        jnp.where(taken, 1.0, 0.0).astype(BF16),
        tokens_ref[...],
        (((0,), (0,)), ((), ())),
        preferred_element_type=F32,
    ).astype(BF16)


def pick_rows(tokens, slots, chunk):
    count = tokens.shape[0]
    return pl.pallas_call(
        pick_kernel,
        grid=(D // chunk,),
        in_specs=[
            pl.BlockSpec((count, chunk), lambda j: (0, j)),
            pl.BlockSpec((count, LANES), lambda j: (0, D // LANES)),
        ],
        out_specs=pl.BlockSpec((1, slots, chunk), lambda j: (j, 0, 0)),
        out_shape=jax.ShapeDtypeStruct((D // chunk, slots, chunk), BF16),
        name="pick",
    )(tokens, tokens)


def combine_kernel(note_ref, rows_ref, out_ref):
    note = note_ref[...].astype(F32)
    share = note[:, 2:3] + note[:, 3:4] + note[:, 4:5]
    slots = lax.broadcasted_iota(jnp.int32, (note.shape[0], rows_ref.shape[1]), 1).astype(F32)
    weight = jnp.where(slots == note[:, 0:1], share, 0.0)
    weight = weight + jnp.where(slots == note[:, 1:2], 1.0 - share, 0.0)
    high = weight.astype(BF16)
    low = (weight - high.astype(F32)).astype(BF16)
    rows = rows_ref[0]
    total = jnp.dot(high, rows, preferred_element_type=F32)
    out_ref[...] = (total + jnp.dot(low, rows, preferred_element_type=F32)).astype(BF16)


def combine_rows(note, rows):
    count = note.shape[0]
    chunks, slots, chunk = rows.shape
    return pl.pallas_call(
        combine_kernel,
        grid=(chunks,),
        in_specs=[
            pl.BlockSpec((count, LANES), lambda j: (0, 0)),
            pl.BlockSpec((1, slots, chunk), lambda j: (j, 0, 0)),
        ],
        out_specs=pl.BlockSpec((count, chunk), lambda j: (0, j)),
        out_shape=jax.ShapeDtypeStruct((count, chunks * chunk), BF16),
        name="combine",
    )(note, rows)


def layer(
    queries,
    keys,
    values,
    out_weight,
    residual,
    norm_gain,
    route_logits,
    expert_ids,
    doc_lengths,
    gate_up_weight,
    down_weight,
):
    xs = lax.axis_size("hidden")
    zl = lax.axis_size(ATTN)
    pairs = lax.axis_size("pair")
    experts = lax.axis_size(("y", "core"))
    capacity = 2
    chunk = D // xs
    z_hi = lax.axis_index("pair")

    unit = gate_up_weight.shape[-1]
    down = down_weight[0].reshape(xs, pairs, unit, -1)
    width = down.shape[-1]
    kept = lax.dynamic_index_in_dim(down, z_hi, 1, keepdims=False)
    sent = lax.dynamic_index_in_dim(down, 1 - z_hi, 1, keepdims=False)

    heads_out = attention(queries[0], keys[0], values[0], doc_lengths[0])
    tok_group = heads_out.shape[0]
    owned = tok_group // (zl * xs)
    projected = jnp.dot(heads_out, out_weight, preferred_element_type=F32).astype(BF16)
    projected = projected.reshape(zl, xs, owned, D).transpose(1, 0, 2, 3)
    projected = jnp.sum(exchange(projected, "hidden").astype(F32), axis=0).astype(BF16)
    gate_up = gate_up_weight[0].reshape(2, xs, chunk, unit)
    me = lax.axis_index("hidden")
    gathered = jnp.zeros((xs, 2, chunk, unit), BF16)
    for d in range(xs):
        block = lax.dynamic_index_in_dim(gate_up, (me + d) % xs, 1, keepdims=False)
        if d > 0:
            block = lax.ppermute(block, "hidden", [(i, (i + d) % xs) for i in range(xs)])
        gathered = lax.dynamic_update_index_in_dim(gathered, block, (me - d) % xs, 0)
    projected = jnp.sum(exchange(projected, ATTN).astype(F32), axis=0)
    gate_up = gathered.transpose(2, 1, 0, 3).reshape(chunk, 2 * xs * unit)
    attended = residual[0].astype(F32) + projected
    scale = lax.rsqrt(jnp.mean(attended * attended, axis=1, keepdims=True) + EPSILON)
    normed = (attended * scale * norm_gain).astype(BF16)

    places = lax.axis_size(Z_AXES)
    chosen = expert_ids[0].reshape(2 * owned)
    slots = slot_numbers(chosen, lax.axis_index(Z_AXES), places, capacity).reshape(owned, 2)
    logits = route_logits[0]
    note = note_of(slots, jax.nn.sigmoid(logits[:, 0] - logits[:, 1]))
    noted = jnp.concatenate([normed, note], axis=1)
    tokens = exchange(jnp.broadcast_to(noted, (places, *noted.shape)), Z_AXES)
    tokens = tokens.reshape(places * owned, D + LANES)
    note = tokens[:, D:]

    group_slots = experts * places * capacity
    picked = pick_rows(tokens, group_slots, chunk)
    picked, sent = lax.optimization_barrier((picked, sent))
    other = lax.ppermute(sent, "pair", [(0, 1), (1, 0)])
    rows = exchange(picked.reshape(xs * experts, -1, chunk), ROUTE).reshape(-1, chunk)

    partial = jnp.dot(rows, gate_up, preferred_element_type=F32).astype(BF16)
    partial = partial.reshape(xs, -1, partial.shape[1])
    summed = jnp.sum(exchange(partial, "hidden").astype(F32), axis=0)
    half = xs * unit
    activated = (jax.nn.silu(summed[:, :half]) * summed[:, half:]).astype(BF16)
    activated = exchange(jnp.broadcast_to(activated, (xs, *activated.shape)), "hidden")
    activated = activated.reshape(-1, half)
    kept = kept.reshape(half, width)
    other = other.reshape(half, width)
    down = jnp.concatenate(
        [jnp.where(z_hi == 0, kept, other), jnp.where(z_hi == 0, other, kept)], axis=1
    )
    out = jnp.dot(activated, down, preferred_element_type=F32).astype(BF16)

    returned = exchange(out.reshape(xs * experts, -1, chunk), ROUTE)
    returned = combine_rows(note, returned.reshape(xs, group_slots, chunk))
    mixed = exchange(returned.reshape(places, owned, D), Z_AXES)
    layer_out = attended + jnp.sum(mixed.astype(F32), axis=0)
    return layer_out.astype(BF16)[None]


def solution(mesh):
    cut = Mesh(
        mesh.devices.reshape(2, 4, 4, 2, 4, 2), ("ab", "aa", "y", "core", "hidden", "pair")
    )
    expert = ("y", "core")
    group = ("y", "core", "pair")
    owner = ("ab", "aa", "hidden")
    in_specs = (
        P(group, None, owner),
        P(group, None, ATTN),
        P(group, None, ATTN),
        P(owner, None),
        P(group, owner, None),
        P(),
        P(group, owner, None),
        P(group, owner, None),
        P(group, None),
        P(expert, None, None, ("ab", "aa", "hidden", "pair")),
        P(expert, ATTN, ("hidden", "pair")),
    )
    return jax.shard_map(
        layer, mesh=cut, in_specs=in_specs, out_specs=P(group, owner, None), check_vma=False
    )
```

```python
import jax
import jax.numpy as jnp
from jax import lax
from jax.experimental import pallas as pl
from jax.sharding import Mesh
from jax.sharding import PartitionSpec as P


D = 4096
HD = 128
EPSILON = 1e-05
BF16 = jnp.bfloat16
F32 = jnp.float32


ATTN = ("ab", "am", "al")
HIDDEN = ("xh", "xl")
QUAD = ("al", "xl")
Z_AXES = ("pair", "ab", "am", "al")
ROUTE = ("xh", "xl", "y", "core")
LANES = 128


def exchange(value, axes):
    return lax.all_to_all(value, axes, 0, 0, tiled=True)


def attention(queries, keys, values, doc_lengths):
    tok_group = queries.shape[0]
    doc_ends = jnp.cumsum(doc_lengths)
    positions = jnp.arange(tok_group, dtype=jnp.int32)
    document = jnp.sum((positions[:, None] >= doc_ends[None, :]).astype(jnp.int32), axis=1)
    allowed = (document[:, None] == document[None, :]) & (positions[None, :] <= positions[:, None])
    scores = jnp.dot(queries, keys.T, preferred_element_type=F32) * HD ** (-0.5)
    scores = jnp.where(allowed, scores, -1e30)
    row_top = jnp.max(scores, axis=1, keepdims=True)
    weights = jnp.exp(scores - row_top)
    probabilities = (weights / jnp.sum(weights, axis=1, keepdims=True)).astype(BF16)
    return jnp.dot(probabilities, values, preferred_element_type=F32).astype(BF16)


def slot_numbers(chosen, place, places, capacity):
    rows = chosen.shape[0]
    row_ids = jnp.arange(rows, dtype=jnp.int32)
    earlier = row_ids[None, :] < row_ids[:, None]
    same = chosen[:, None] == chosen[None, :]
    ranking = jnp.sum((same & earlier).astype(jnp.int32), axis=-1)
    return (chosen * places + place) * capacity + ranking


def note_of(slots, share):
    high = lax.reduce_precision(share, 8, 7)
    middle = lax.reduce_precision(share - high, 8, 7)
    low = share - high - middle
    parts = jnp.stack([slots[:, 0].astype(F32), slots[:, 1].astype(F32), high, middle, low], axis=1)
    return jnp.pad(parts, ((0, 0), (0, LANES - 5))).astype(BF16)


def pick_kernel(tokens_ref, note_ref, out_ref):
    note = note_ref[...].astype(F32)
    slots = lax.broadcasted_iota(jnp.int32, (note.shape[0], out_ref.shape[1]), 1).astype(F32)
    taken = (slots == note[:, 0:1]) | (slots == note[:, 1:2])
    out_ref[0] = lax.dot_general(
        jnp.where(taken, 1.0, 0.0).astype(BF16),
        tokens_ref[...],
        (((0,), (0,)), ((), ())),
        preferred_element_type=F32,
    ).astype(BF16)


def pick_rows(tokens, slots, chunk, copies):
    count = tokens.shape[0]
    width = tokens.shape[1] - LANES
    parts = width // chunk
    return pl.pallas_call(
        pick_kernel,
        grid=(copies * parts,),
        in_specs=[
            pl.BlockSpec((count, chunk), lambda j: (0, j % parts)),
            pl.BlockSpec((count, LANES), lambda j: (0, width // LANES)),
        ],
        out_specs=pl.BlockSpec((1, slots, chunk), lambda j: (j, 0, 0)),
        out_shape=jax.ShapeDtypeStruct((copies * parts, slots, chunk), BF16),
        name="pick",
    )(tokens, tokens)


def combine_kernel(note_ref, rows_ref, out_ref):
    note = note_ref[...].astype(F32)
    share = note[:, 2:3] + note[:, 3:4] + note[:, 4:5]
    slots = lax.broadcasted_iota(jnp.int32, (note.shape[0], rows_ref.shape[2]), 1).astype(F32)
    weight = jnp.where(slots == note[:, 0:1], share, 0.0)
    weight = weight + jnp.where(slots == note[:, 1:2], 1.0 - share, 0.0)
    high = weight.astype(BF16)
    low = (weight - high.astype(F32)).astype(BF16)
    total = jnp.zeros(out_ref.shape, F32)
    for k in range(rows_ref.shape[0]):
        rows = rows_ref[k, 0]
        total += jnp.dot(high, rows, preferred_element_type=F32)
        total += jnp.dot(low, rows, preferred_element_type=F32)
    out_ref[...] = total.astype(BF16)


def combine_rows(note, rows):
    count = note.shape[0]
    sums, chunks, slots, chunk = rows.shape
    return pl.pallas_call(
        combine_kernel,
        grid=(chunks,),
        in_specs=[
            pl.BlockSpec((count, LANES), lambda j: (0, 0)),
            pl.BlockSpec((sums, 1, slots, chunk), lambda j: (0, j, 0, 0)),
        ],
        out_specs=pl.BlockSpec((count, chunk), lambda j: (0, j)),
        out_shape=jax.ShapeDtypeStruct((count, chunks * chunk), BF16),
        name="combine",
    )(note, rows)


def down_moves(i, j):
    moves = []
    for high in range(4):
        for n in range(16):
            al, xh, xl, pair = n >> 3, (n >> 2) & 1, (n >> 1) & 1, n & 1
            moves.append((high * 16 + n, high * 16 + xh * 8 + (al ^ i) * 4 + xl * 2 + (pair ^ j)))
    return moves


def layer(
    queries,
    keys,
    values,
    out_weight,
    residual,
    norm_gain,
    route_logits,
    expert_ids,
    doc_lengths,
    gate_up_weight,
    down_weight,
):
    xs = lax.axis_size(HIDDEN)
    zl = lax.axis_size(ATTN)
    pairs = lax.axis_size("pair")
    experts = lax.axis_size(("y", "core"))
    quad = lax.axis_size(QUAD)
    capacity = 2
    chunk = D // quad
    unit = gate_up_weight.shape[-1]
    half = quad * unit

    heads_out = attention(queries[0], keys[0], values[0], doc_lengths[0])
    tok_group = heads_out.shape[0]
    owned = tok_group // (zl * xs)
    projected = jnp.dot(heads_out, out_weight, preferred_element_type=F32).astype(BF16)
    projected = projected.reshape(zl, xs, owned, D).transpose(1, 0, 2, 3)
    projected = jnp.sum(exchange(projected, HIDDEN).astype(F32), axis=0).astype(BF16)
    me = lax.axis_index(QUAD)
    gate_up = gate_up_weight[0].reshape(2, quad, chunk, unit)
    gathered = jnp.zeros((quad, 2, chunk, unit), BF16)
    for d in range(quad):
        block = lax.dynamic_index_in_dim(gate_up, me ^ d, 1, keepdims=False)
        if d > 0:
            block = lax.ppermute(block, QUAD, [(i, i ^ d) for i in range(quad)])
        gathered = lax.dynamic_update_index_in_dim(gathered, block, me ^ d, 0)
    projected = jnp.sum(exchange(projected, ATTN).astype(F32), axis=0)
    gate_up = gathered.transpose(2, 1, 0, 3).reshape(chunk, 2 * half)
    attended = residual[0].astype(F32) + projected
    scale = lax.rsqrt(jnp.mean(attended * attended, axis=1, keepdims=True) + EPSILON)
    normed = (attended * scale * norm_gain).astype(BF16)

    places = lax.axis_size(Z_AXES)
    chosen = expert_ids[0].reshape(2 * owned)
    slots = slot_numbers(chosen, lax.axis_index(Z_AXES), places, capacity).reshape(owned, 2)
    logits = route_logits[0]
    note = note_of(slots, jax.nn.sigmoid(logits[:, 0] - logits[:, 1]))
    parity = lax.axis_size("al")
    width = D // parity
    noted = jnp.stack(
        [jnp.concatenate([normed[:, k * width : (k + 1) * width], note], axis=1) for k in range(parity)]
    )
    noted = jnp.broadcast_to(noted, (places // parity, *noted.shape))
    tokens = exchange(noted.reshape(places, owned, width + LANES), Z_AXES)
    tokens = tokens.reshape(places * owned, width + LANES)
    note = tokens[:, width:]

    group_slots = experts * places * capacity
    picked = pick_rows(tokens, group_slots, chunk, lax.axis_size("xh"))
    blocks = down_weight[0].reshape(2, 2, pairs, unit, -1)
    part = blocks.shape[-1]
    picked, blocks = lax.optimization_barrier((picked, blocks))
    al, xh, z_hi = lax.axis_index("al"), lax.axis_index("xh"), lax.axis_index("pair")
    down = jnp.zeros((parity, 2 * unit, pairs * part), BF16)
    for i, j in ((0, 1), (1, 1), (0, 0), (1, 0)):
        sent = lax.dynamic_slice(
            blocks, (al ^ i, 0, z_hi ^ j, 0, 0), (1, 2, 1, unit, part)
        ).reshape(2 * unit, part)
        sent = lax.ppermute(sent, ("ab", "am", "al", "xh", "xl", "pair"), down_moves(i, j))
        down = lax.dynamic_update_slice(down, sent[None], (xh ^ i, 0, (z_hi ^ j) * part))
    down = down.reshape(half, chunk)
    rows = exchange(picked.reshape(xs * experts, -1, chunk), ROUTE).reshape(-1, chunk)

    partial = jnp.dot(rows, gate_up, preferred_element_type=F32).astype(BF16)
    partial = partial.reshape(quad, -1, partial.shape[1])
    summed = jnp.sum(exchange(partial, QUAD).astype(F32), axis=0)
    activated = (jax.nn.silu(summed[:, :half]) * summed[:, half:]).astype(BF16)
    activated = exchange(jnp.broadcast_to(activated, (quad, *activated.shape)), QUAD)
    activated = activated.reshape(-1, half)
    out = jnp.dot(activated, down, preferred_element_type=F32).astype(BF16)

    returned = exchange(out.reshape(xs * experts, -1, chunk), ROUTE)
    returned = combine_rows(note, returned.reshape(2, 2, group_slots, chunk))
    mixed = exchange(returned.reshape(places, owned, width), Z_AXES)
    mixed = jnp.sum(mixed.reshape(-1, parity, owned, width).astype(F32), axis=0)
    layer_out = attended + jnp.concatenate([mixed[k] for k in range(parity)], axis=1)
    return layer_out.astype(BF16)[None]


def solution(mesh):
    cut = Mesh(
        mesh.devices.reshape(2, 2, 2, 4, 2, 2, 2, 2),
        ("ab", "am", "al", "y", "core", "xh", "xl", "pair"),
    )
    expert = ("y", "core")
    group = ("y", "core", "pair")
    owner = (*ATTN, *HIDDEN)
    in_specs = (
        P(group, None, owner),
        P(group, None, ATTN),
        P(group, None, ATTN),
        P(owner, None),
        P(group, owner, None),
        P(),
        P(group, owner, None),
        P(group, owner, None),
        P(group, None),
        P(expert, None, None, (*owner, "pair")),
        P(expert, ATTN, (*HIDDEN, "pair")),
    )
    return jax.shard_map(
        layer, mesh=cut, in_specs=in_specs, out_specs=P(group, owner, None), check_vma=False
    )
```

```python
import jax
import jax.numpy as jnp
from jax import lax
from jax.experimental import pallas as pl
from jax.sharding import Mesh
from jax.sharding import PartitionSpec as P


D = 4096
HD = 128
EPSILON = 1e-05
BF16 = jnp.bfloat16
F32 = jnp.float32


ATTN = ("ab", "am", "al")
HIDDEN = ("xh", "xl")
Z_AXES = ("pair", "ab", "am", "al")
ROUTE = ("xh", "xl", "y", "core")
LANES = 128


def exchange(value, axes):
    return lax.all_to_all(value, axes, 0, 0, tiled=True)


def attention(queries, keys, values, doc_lengths):
    tok_group = queries.shape[0]
    doc_ends = jnp.cumsum(doc_lengths)
    positions = jnp.arange(tok_group, dtype=jnp.int32)
    document = jnp.sum((positions[:, None] >= doc_ends[None, :]).astype(jnp.int32), axis=1)
    allowed = (document[:, None] == document[None, :]) & (positions[None, :] <= positions[:, None])
    scores = jnp.dot(queries, keys.T, preferred_element_type=F32) * HD ** (-0.5)
    scores = jnp.where(allowed, scores, -1e30)
    row_top = jnp.max(scores, axis=1, keepdims=True)
    weights = jnp.exp(scores - row_top)
    probabilities = (weights / jnp.sum(weights, axis=1, keepdims=True)).astype(BF16)
    return jnp.dot(probabilities, values, preferred_element_type=F32).astype(BF16)


def slot_numbers(chosen, place, places, capacity):
    rows = chosen.shape[0]
    row_ids = jnp.arange(rows, dtype=jnp.int32)
    earlier = row_ids[None, :] < row_ids[:, None]
    same = chosen[:, None] == chosen[None, :]
    ranking = jnp.sum((same & earlier).astype(jnp.int32), axis=-1)
    return (chosen * places + place) * capacity + ranking


def note_of(slots, share):
    high = lax.reduce_precision(share, 8, 7)
    middle = lax.reduce_precision(share - high, 8, 7)
    low = share - high - middle
    parts = jnp.stack([slots[:, 0].astype(F32), slots[:, 1].astype(F32), high, middle, low], axis=1)
    return jnp.pad(parts, ((0, 0), (0, LANES - 5))).astype(BF16)


def pick_kernel(tokens_ref, note_ref, out_ref):
    note = note_ref[...].astype(F32)
    slots = lax.broadcasted_iota(jnp.int32, (note.shape[0], out_ref.shape[1]), 1).astype(F32)
    taken = (slots == note[:, 0:1]) | (slots == note[:, 1:2])
    out_ref[0] = lax.dot_general(
        jnp.where(taken, 1.0, 0.0).astype(BF16),
        tokens_ref[...],
        (((0,), (0,)), ((), ())),
        preferred_element_type=F32,
    ).astype(BF16)


def pick_rows(tokens, slots, chunk):
    count = tokens.shape[0]
    return pl.pallas_call(
        pick_kernel,
        grid=(D // chunk,),
        in_specs=[
            pl.BlockSpec((count, chunk), lambda j: (0, j)),
            pl.BlockSpec((count, LANES), lambda j: (0, D // LANES)),
        ],
        out_specs=pl.BlockSpec((1, slots, chunk), lambda j: (j, 0, 0)),
        out_shape=jax.ShapeDtypeStruct((D // chunk, slots, chunk), BF16),
        name="pick",
    )(tokens, tokens)


def combine_kernel(note_ref, rows_ref, out_ref):
    note = note_ref[...].astype(F32)
    share = note[:, 2:3] + note[:, 3:4] + note[:, 4:5]
    slots = lax.broadcasted_iota(jnp.int32, (note.shape[0], rows_ref.shape[2]), 1).astype(F32)
    weight = jnp.where(slots == note[:, 0:1], share, 0.0)
    weight = weight + jnp.where(slots == note[:, 1:2], 1.0 - share, 0.0)
    high = weight.astype(BF16)
    low = (weight - high.astype(F32)).astype(BF16)
    total = jnp.zeros(out_ref.shape, F32)
    for k in range(rows_ref.shape[0]):
        rows = rows_ref[k, 0]
        total += jnp.dot(high, rows, preferred_element_type=F32)
        total += jnp.dot(low, rows, preferred_element_type=F32)
    out_ref[...] = total.astype(BF16)


def combine_rows(note, rows):
    count = note.shape[0]
    sums, chunks, slots, chunk = rows.shape
    return pl.pallas_call(
        combine_kernel,
        grid=(chunks,),
        in_specs=[
            pl.BlockSpec((count, LANES), lambda j: (0, 0)),
            pl.BlockSpec((sums, 1, slots, chunk), lambda j: (0, j, 0, 0)),
        ],
        out_specs=pl.BlockSpec((count, chunk), lambda j: (0, j)),
        out_shape=jax.ShapeDtypeStruct((count, chunks * chunk), BF16),
        name="combine",
    )(note, rows)


def down_moves(i, j):
    moves = []
    for high in range(4):
        for n in range(16):
            al, xh, xl, pair = n >> 3, (n >> 2) & 1, (n >> 1) & 1, n & 1
            moves.append((high * 16 + n, high * 16 + xh * 8 + (al ^ i) * 4 + xl * 2 + (pair ^ j)))
    return moves


def layer(
    queries,
    keys,
    values,
    out_weight,
    residual,
    norm_gain,
    route_logits,
    expert_ids,
    doc_lengths,
    gate_up_weight,
    down_weight,
):
    xs = lax.axis_size(HIDDEN)
    zl = lax.axis_size(ATTN)
    pairs = lax.axis_size("pair")
    experts = lax.axis_size(("y", "core"))
    capacity = 2
    chunk = D // xs
    unit = gate_up_weight.shape[-1]
    half = xs * unit

    heads_out = attention(queries[0], keys[0], values[0], doc_lengths[0])
    tok_group = heads_out.shape[0]
    owned = tok_group // (zl * xs)
    projected = jnp.dot(heads_out, out_weight, preferred_element_type=F32).astype(BF16)
    projected = projected.reshape(zl, xs, owned, D).transpose(1, 0, 2, 3)
    projected = jnp.sum(exchange(projected, HIDDEN).astype(F32), axis=0).astype(BF16)
    me = lax.axis_index(HIDDEN)
    gate_up = gate_up_weight[0].reshape(2, xs, chunk, unit)
    gathered = jnp.zeros((xs, 2, chunk, unit), BF16)
    for d in range(xs):
        block = lax.dynamic_index_in_dim(gate_up, me ^ d, 1, keepdims=False)
        if d > 0:
            block = lax.ppermute(block, HIDDEN, [(i, i ^ d) for i in range(xs)])
        gathered = lax.dynamic_update_index_in_dim(gathered, block, me ^ d, 0)
    projected = jnp.sum(exchange(projected, ATTN).astype(F32), axis=0)
    gate_up = gathered.transpose(2, 1, 0, 3).reshape(chunk, 2 * half)
    attended = residual[0].astype(F32) + projected
    scale = lax.rsqrt(jnp.mean(attended * attended, axis=1, keepdims=True) + EPSILON)
    normed = (attended * scale * norm_gain).astype(BF16)

    places = lax.axis_size(Z_AXES)
    chosen = expert_ids[0].reshape(2 * owned)
    slots = slot_numbers(chosen, lax.axis_index(Z_AXES), places, capacity).reshape(owned, 2)
    logits = route_logits[0]
    note = note_of(slots, jax.nn.sigmoid(logits[:, 0] - logits[:, 1]))
    noted = jnp.concatenate([normed, note], axis=1)
    tokens = exchange(jnp.broadcast_to(noted, (places, *noted.shape)), Z_AXES)
    tokens = tokens.reshape(places * owned, D + LANES)
    note = tokens[:, D:]

    group_slots = experts * places * capacity
    picked = pick_rows(tokens, group_slots, chunk)
    parity = lax.axis_size("al")
    blocks = down_weight[0].reshape(2, 2, pairs, unit, -1)
    part = blocks.shape[-1]
    picked, blocks = lax.optimization_barrier((picked, blocks))
    al, xh, z_hi = lax.axis_index("al"), lax.axis_index("xh"), lax.axis_index("pair")
    down = jnp.zeros((parity, 2 * unit, pairs * part), BF16)
    for i, j in ((0, 1), (1, 1), (0, 0), (1, 0)):
        sent = lax.dynamic_slice(
            blocks, (al ^ i, 0, z_hi ^ j, 0, 0), (1, 2, 1, unit, part)
        ).reshape(2 * unit, part)
        sent = lax.ppermute(sent, ("ab", "am", "al", "xh", "xl", "pair"), down_moves(i, j))
        down = lax.dynamic_update_slice(down, sent[None], (xh ^ i, 0, (z_hi ^ j) * part))
    rows = exchange(picked.reshape(xs * experts, -1, chunk), ROUTE).reshape(-1, chunk)

    partial = jnp.dot(rows, gate_up, preferred_element_type=F32).astype(BF16)
    partial = partial.reshape(xs, -1, partial.shape[1])
    summed = jnp.sum(exchange(partial, HIDDEN).astype(F32), axis=0)
    activated = (jax.nn.silu(summed[:, :half]) * summed[:, half:]).astype(BF16)
    activated = jnp.stack([activated[:, : half // 2], activated[:, half // 2 :]])[None, :, None]
    activated = jnp.broadcast_to(activated, (parity, 2, 2, *activated.shape[3:]))
    activated = activated.reshape(parity * xs, *activated.shape[3:])
    activated = exchange(activated, ("al", *HIDDEN)).reshape(parity, -1, half // 2)
    activated = jnp.concatenate([activated[k] for k in range(parity)], axis=1)
    out = jnp.dot(activated, down.reshape(half, chunk), preferred_element_type=F32).astype(BF16)

    returned = exchange(out.reshape(xs * experts, -1, chunk), ROUTE)
    returned = combine_rows(note, returned.reshape(2, 2, group_slots, chunk))
    width = D // parity
    mixed = exchange(returned.reshape(places, owned, width), Z_AXES)
    mixed = jnp.sum(mixed.reshape(-1, parity, owned, width).astype(F32), axis=0)
    layer_out = attended + jnp.concatenate([mixed[k] for k in range(parity)], axis=1)
    return layer_out.astype(BF16)[None]


def solution(mesh):
    cut = Mesh(
        mesh.devices.reshape(2, 2, 2, 4, 2, 2, 2, 2),
        ("ab", "am", "al", "y", "core", "xh", "xl", "pair"),
    )
    expert = ("y", "core")
    group = ("y", "core", "pair")
    owner = (*ATTN, *HIDDEN)
    in_specs = (
        P(group, None, owner),
        P(group, None, ATTN),
        P(group, None, ATTN),
        P(owner, None),
        P(group, owner, None),
        P(),
        P(group, owner, None),
        P(group, owner, None),
        P(group, None),
        P(expert, None, None, (*owner, "pair")),
        P(expert, ATTN, (*HIDDEN, "pair")),
    )
    return jax.shard_map(
        layer, mesh=cut, in_specs=in_specs, out_specs=P(group, owner, None), check_vma=False
    )
```

```python
import jax
import jax.numpy as jnp
from jax import lax
from jax.experimental import pallas as pl
from jax.sharding import Mesh
from jax.sharding import PartitionSpec as P


D = 4096
HD = 128
EPSILON = 1e-05
BF16 = jnp.bfloat16
F32 = jnp.float32


ATTN = ("ab", "am", "al")
Z_AXES = ("pair", "ab", "am")
ROUTE = ("al", "hidden", "y", "core")
LANES = 128


def exchange(value, axes):
    return lax.all_to_all(value, axes, 0, 0, tiled=True)


def attention(queries, keys, values, doc_lengths):
    tok_group = queries.shape[0]
    doc_ends = jnp.cumsum(doc_lengths)
    positions = jnp.arange(tok_group, dtype=jnp.int32)
    document = jnp.sum((positions[:, None] >= doc_ends[None, :]).astype(jnp.int32), axis=1)
    allowed = (document[:, None] == document[None, :]) & (positions[None, :] <= positions[:, None])
    scores = jnp.dot(queries, keys.T, preferred_element_type=F32) * HD ** (-0.5)
    scores = jnp.where(allowed, scores, -1e30)
    row_top = jnp.max(scores, axis=1, keepdims=True)
    weights = jnp.exp(scores - row_top)
    probabilities = (weights / jnp.sum(weights, axis=1, keepdims=True)).astype(BF16)
    return jnp.dot(probabilities, values, preferred_element_type=F32).astype(BF16)


def slot_numbers(chosen, place, places, capacity):
    rows = chosen.shape[0]
    row_ids = jnp.arange(rows, dtype=jnp.int32)
    earlier = row_ids[None, :] < row_ids[:, None]
    same = chosen[:, None] == chosen[None, :]
    ranking = jnp.sum((same & earlier).astype(jnp.int32), axis=-1)
    return (chosen * places + place) * capacity + ranking


def note_of(slots, share):
    high = lax.reduce_precision(share, 8, 7)
    middle = lax.reduce_precision(share - high, 8, 7)
    low = share - high - middle
    parts = jnp.stack([slots[:, 0].astype(F32), slots[:, 1].astype(F32), high, middle, low], axis=1)
    return jnp.pad(parts, ((0, 0), (0, LANES - 5))).astype(BF16)


def pick_kernel(tokens_ref, note_ref, out_ref):
    note = note_ref[...].astype(F32)
    slots = lax.broadcasted_iota(jnp.int32, (note.shape[0], out_ref.shape[1]), 1).astype(F32)
    taken = (slots == note[:, 0:1]) | (slots == note[:, 1:2])
    out_ref[0] = lax.dot_general(
        jnp.where(taken, 1.0, 0.0).astype(BF16),
        tokens_ref[...],
        (((0,), (0,)), ((), ())),
        preferred_element_type=F32,
    ).astype(BF16)


def pick_rows(tokens, slots, chunk, copies):
    count = tokens.shape[0]
    parts = D // chunk
    return pl.pallas_call(
        pick_kernel,
        grid=(copies * parts,),
        in_specs=[
            pl.BlockSpec((count, chunk), lambda j: (0, j % parts)),
            pl.BlockSpec((count, LANES), lambda j: (0, D // LANES)),
        ],
        out_specs=pl.BlockSpec((1, slots, chunk), lambda j: (j, 0, 0)),
        out_shape=jax.ShapeDtypeStruct((copies * parts, slots, chunk), BF16),
        name="pick",
    )(tokens, tokens)


def combine_kernel(note_ref, rows_ref, out_ref):
    note = note_ref[...].astype(F32)
    share = note[:, 2:3] + note[:, 3:4] + note[:, 4:5]
    slots = lax.broadcasted_iota(jnp.int32, (note.shape[0], rows_ref.shape[2]), 1).astype(F32)
    weight = jnp.where(slots == note[:, 0:1], share, 0.0)
    weight = weight + jnp.where(slots == note[:, 1:2], 1.0 - share, 0.0)
    high = weight.astype(BF16)
    low = (weight - high.astype(F32)).astype(BF16)
    total = jnp.zeros(out_ref.shape, F32)
    for k in range(rows_ref.shape[0]):
        rows = rows_ref[k, 0]
        total += jnp.dot(high, rows, preferred_element_type=F32)
        total += jnp.dot(low, rows, preferred_element_type=F32)
    out_ref[...] = total.astype(BF16)


def combine_rows(note, rows):
    count = note.shape[0]
    sums, chunks, slots, chunk = rows.shape
    return pl.pallas_call(
        combine_kernel,
        grid=(chunks,),
        in_specs=[
            pl.BlockSpec((count, LANES), lambda j: (0, 0)),
            pl.BlockSpec((sums, 1, slots, chunk), lambda j: (0, j, 0, 0)),
        ],
        out_specs=pl.BlockSpec((count, chunk), lambda j: (0, j)),
        out_shape=jax.ShapeDtypeStruct((count, chunks * chunk), BF16),
        name="combine",
    )(note, rows)


def layer(
    queries,
    keys,
    values,
    out_weight,
    residual,
    norm_gain,
    route_logits,
    expert_ids,
    doc_lengths,
    gate_up_weight,
    down_weight,
):
    xs = lax.axis_size("hidden")
    zl = lax.axis_size(ATTN)
    pairs = lax.axis_size("pair")
    experts = lax.axis_size(("y", "core"))
    capacity = 2
    chunk = D // xs
    z_hi = lax.axis_index("pair")

    unit = gate_up_weight.shape[-1]
    down = down_weight[0].reshape(xs, pairs, unit, -1)
    width = down.shape[-1]
    kept = lax.dynamic_index_in_dim(down, z_hi, 1, keepdims=False)
    sent = lax.dynamic_index_in_dim(down, 1 - z_hi, 1, keepdims=False)

    heads_out = attention(queries[0], keys[0], values[0], doc_lengths[0])
    tok_group = heads_out.shape[0]
    owned = tok_group // (zl * xs)
    projected = jnp.dot(heads_out, out_weight, preferred_element_type=F32).astype(BF16)
    projected = projected.reshape(zl, xs, owned, D).transpose(1, 0, 2, 3)
    projected = jnp.sum(exchange(projected, "hidden").astype(F32), axis=0).astype(BF16)
    gate_up = gate_up_weight[0].reshape(2, xs, chunk, unit)
    me = lax.axis_index("hidden")
    gathered = jnp.zeros((xs, 2, chunk, unit), BF16)
    for d in range(xs):
        block = lax.dynamic_index_in_dim(gate_up, (me + d) % xs, 1, keepdims=False)
        if d > 0:
            block = lax.ppermute(block, "hidden", [(i, (i + d) % xs) for i in range(xs)])
        gathered = lax.dynamic_update_index_in_dim(gathered, block, (me - d) % xs, 0)
    projected = jnp.sum(exchange(projected, ATTN).astype(F32), axis=0)
    gate_up = gathered.transpose(2, 1, 0, 3).reshape(chunk, 2 * xs * unit)
    attended = residual[0].astype(F32) + projected
    scale = lax.rsqrt(jnp.mean(attended * attended, axis=1, keepdims=True) + EPSILON)
    normed = (attended * scale * norm_gain).astype(BF16)

    places = lax.axis_size(Z_AXES)
    chosen = expert_ids[0].reshape(2 * owned)
    slots = slot_numbers(chosen, lax.axis_index(Z_AXES), places, capacity).reshape(owned, 2)
    logits = route_logits[0]
    note = note_of(slots, jax.nn.sigmoid(logits[:, 0] - logits[:, 1]))
    noted = jnp.concatenate([normed, note], axis=1)
    tokens = exchange(jnp.broadcast_to(noted, (places, *noted.shape)), Z_AXES)
    tokens = tokens.reshape(places * owned, D + LANES)
    note = tokens[:, D:]

    group_slots = experts * places * capacity
    parities = lax.axis_size("al")
    picked = pick_rows(tokens, group_slots, chunk, parities)
    picked, sent = lax.optimization_barrier((picked, sent))
    other = lax.ppermute(sent, "pair", [(0, 1), (1, 0)])
    rows = exchange(picked.reshape(parities * xs * experts, -1, chunk), ROUTE).reshape(-1, chunk)

    partial = jnp.dot(rows, gate_up, preferred_element_type=F32).astype(BF16)
    partial = partial.reshape(xs, -1, partial.shape[1])
    summed = jnp.sum(exchange(partial, "hidden").astype(F32), axis=0)
    half = xs * unit
    activated = (jax.nn.silu(summed[:, :half]) * summed[:, half:]).astype(BF16)
    activated = exchange(jnp.broadcast_to(activated, (xs, *activated.shape)), "hidden")
    activated = activated.reshape(-1, half)
    kept = kept.reshape(half, width)
    other = other.reshape(half, width)
    down = jnp.concatenate(
        [jnp.where(z_hi == 0, kept, other), jnp.where(z_hi == 0, other, kept)], axis=1
    )
    out = jnp.dot(activated, down, preferred_element_type=F32).astype(BF16)

    returned = exchange(out.reshape(parities * xs * experts, -1, chunk), ROUTE)
    returned = combine_rows(note, returned.reshape(parities, xs, group_slots, chunk))
    mixed = exchange(returned.reshape(places, owned, D), Z_AXES)
    layer_out = attended + jnp.sum(mixed.astype(F32), axis=0)
    return layer_out.astype(BF16)[None]


def solution(mesh):
    cut = Mesh(
        mesh.devices.reshape(2, 2, 2, 4, 2, 4, 2),
        ("ab", "am", "al", "y", "core", "hidden", "pair"),
    )
    expert = ("y", "core")
    group = ("y", "core", "pair")
    owner = (*ATTN, "hidden")
    in_specs = (
        P(group, None, owner),
        P(group, None, ATTN),
        P(group, None, ATTN),
        P(owner, None),
        P(group, owner, None),
        P(),
        P(group, owner, None),
        P(group, owner, None),
        P(group, None),
        P(expert, None, None, (*owner, "pair")),
        P(expert, ATTN, ("hidden", "pair")),
    )
    return jax.shard_map(
        layer, mesh=cut, in_specs=in_specs, out_specs=P(group, owner, None), check_vma=False
    )
```

```python
import jax
import jax.numpy as jnp
from jax import lax
from jax.experimental import pallas as pl
from jax.experimental.pallas import tpu as pltpu
from jax.sharding import Mesh
from jax.sharding import PartitionSpec as P


D = 4096
HD = 128
EPSILON = 1e-05
BF16 = jnp.bfloat16
F32 = jnp.float32


ATTN = ("ab", "am", "al")
Z_AXES = ("pair", "ab", "am")
ROUTE = ("al", "hidden", "y", "core")
LANES = 128


def exchange(value, axes):
    return lax.all_to_all(value, axes, 0, 0, tiled=True)


def attention_kernel(doc_ref, queries_ref, keys_ref, values_ref, weight_ref, out_ref):
    count = queries_ref.shape[0]
    first_end = doc_ref[0]
    second_end = first_end + doc_ref[1]
    rows = lax.broadcasted_iota(jnp.int32, (count, count), 0)
    cols = lax.broadcasted_iota(jnp.int32, (count, count), 1)
    row_doc = (rows >= first_end).astype(jnp.int32) + (rows >= second_end).astype(jnp.int32)
    col_doc = (cols >= first_end).astype(jnp.int32) + (cols >= second_end).astype(jnp.int32)
    allowed = (row_doc == col_doc) & (cols <= rows)
    scores = lax.dot_general(
        queries_ref[...],
        keys_ref[...],
        (((1,), (1,)), ((), ())),
        preferred_element_type=F32,
    )
    scores = jnp.where(allowed, scores * HD ** (-0.5), -1e30)
    weights = jnp.exp(scores - jnp.max(scores, axis=1, keepdims=True))
    probabilities = (weights / jnp.sum(weights, axis=1, keepdims=True)).astype(BF16)
    heads_out = jnp.dot(probabilities, values_ref[...], preferred_element_type=F32).astype(BF16)
    total = jnp.dot(heads_out, weight_ref[...], preferred_element_type=F32)
    parts, groups, owned, _ = out_ref.shape
    places = parts // 2
    for group in range(groups):
        for part in range(parts):
            start = ((group * 2 + part // places) * places + part % places) * owned
            out_ref[part, group] = total[start : start + owned].astype(BF16)


def attention(doc_lengths, queries, keys, values, out_weight, parts, owned):
    count = queries.shape[0]
    vmem = pl.BlockSpec(memory_space=pltpu.VMEM)
    return pl.pallas_call(
        attention_kernel,
        in_specs=[pl.BlockSpec(memory_space=pltpu.SMEM), vmem, vmem, vmem, vmem],
        out_specs=vmem,
        out_shape=jax.ShapeDtypeStruct((parts, count // (parts * owned), owned, D), BF16),
        name="attention",
    )(doc_lengths, queries, keys, values, out_weight)


def slot_numbers(chosen, place, places, capacity):
    rows = chosen.shape[0]
    row_ids = jnp.arange(rows, dtype=jnp.int32)
    earlier = row_ids[None, :] < row_ids[:, None]
    same = chosen[:, None] == chosen[None, :]
    ranking = jnp.sum((same & earlier).astype(jnp.int32), axis=-1)
    return (chosen * places + place) * capacity + ranking


def note_of(slots, share):
    high = lax.reduce_precision(share, 8, 7)
    middle = lax.reduce_precision(share - high, 8, 7)
    low = share - high - middle
    parts = jnp.stack([slots[:, 0].astype(F32), slots[:, 1].astype(F32), high, middle, low], axis=1)
    return jnp.pad(parts, ((0, 0), (0, LANES - 5))).astype(BF16)


def pick_kernel(tokens_ref, note_ref, out_ref):
    note = note_ref[...].astype(F32)
    slots = lax.broadcasted_iota(jnp.int32, (note.shape[0], out_ref.shape[2]), 1).astype(F32)
    taken = (slots == note[:, 0:1]) | (slots == note[:, 1:2])
    rows = lax.dot_general(
        jnp.where(taken, 1.0, 0.0).astype(BF16),
        tokens_ref[...],
        (((0,), (0,)), ((), ())),
        preferred_element_type=F32,
    ).astype(BF16)
    for copy in range(out_ref.shape[0]):
        out_ref[copy, 0] = rows


def pick_rows(tokens, slots, chunk, copies):
    count = tokens.shape[0]
    return pl.pallas_call(
        pick_kernel,
        grid=(D // chunk,),
        in_specs=[
            pl.BlockSpec((count, chunk), lambda j: (0, j)),
            pl.BlockSpec((count, LANES), lambda j: (0, D // LANES)),
        ],
        out_specs=pl.BlockSpec((copies, 1, slots, chunk), lambda j: (0, j, 0, 0)),
        out_shape=jax.ShapeDtypeStruct((copies, D // chunk, slots, chunk), BF16),
        name="pick",
    )(tokens, tokens)


def combine_kernel(note_ref, rows_ref, out_ref):
    note = note_ref[...].astype(F32)
    share = note[:, 2:3] + note[:, 3:4] + note[:, 4:5]
    slots = lax.broadcasted_iota(jnp.int32, (note.shape[0], rows_ref.shape[2]), 1).astype(F32)
    weight = jnp.where(slots == note[:, 0:1], share, 0.0)
    weight = weight + jnp.where(slots == note[:, 1:2], 1.0 - share, 0.0)
    high = weight.astype(BF16)
    low = (weight - high.astype(F32)).astype(BF16)
    both = jnp.concatenate([high, low], axis=0)
    total = jnp.zeros((2 * note.shape[0], out_ref.shape[2]), F32)
    for k in range(rows_ref.shape[0]):
        total += jnp.dot(both, rows_ref[k, 0], preferred_element_type=F32)
    total = total[: note.shape[0]] + total[note.shape[0] :]
    places, owned, _ = out_ref.shape
    for place in range(places):
        out_ref[place] = total[place * owned : (place + 1) * owned].astype(BF16)


def combine_rows(note, rows, owned):
    count = note.shape[0]
    sums, chunks, slots, chunk = rows.shape
    places = count // owned
    return pl.pallas_call(
        combine_kernel,
        grid=(chunks,),
        in_specs=[
            pl.BlockSpec((count, LANES), lambda j: (0, 0)),
            pl.BlockSpec((sums, 1, slots, chunk), lambda j: (0, j, 0, 0)),
        ],
        out_specs=pl.BlockSpec((places, owned, chunk), lambda j: (0, 0, j)),
        out_shape=jax.ShapeDtypeStruct((places, owned, chunks * chunk), BF16),
        name="combine",
    )(note, rows)


def layer(
    queries,
    keys,
    values,
    out_weight,
    residual,
    norm_gain,
    route_logits,
    expert_ids,
    doc_lengths,
    gate_up_weight,
    down_weight,
):
    xs = lax.axis_size("hidden")
    zl = lax.axis_size(ATTN)
    parities = lax.axis_size("al")
    pairs = lax.axis_size("pair")
    experts = lax.axis_size(("y", "core"))
    capacity = 2
    chunk = D // xs
    z_hi = lax.axis_index("pair")

    unit = gate_up_weight.shape[-1]
    down = down_weight[0].reshape(xs, pairs, unit, -1)
    width = down.shape[-1]
    kept = lax.dynamic_index_in_dim(down, z_hi, 1, keepdims=False)
    sent = lax.dynamic_index_in_dim(down, 1 - z_hi, 1, keepdims=False)

    tok_group = queries.shape[1]
    owned = tok_group // (zl * xs)
    projected = attention(
        doc_lengths[0], queries[0], keys[0], values[0], out_weight, parities * xs, owned
    )
    projected = exchange(projected, ("al", "hidden"))
    projected = jnp.sum(projected.astype(F32), axis=0).astype(BF16)
    gate_up = gate_up_weight[0].reshape(2, xs, chunk, unit)
    me = lax.axis_index("hidden")
    gathered = jnp.zeros((xs, 2, chunk, unit), BF16)
    for d in range(xs):
        block = lax.dynamic_index_in_dim(gate_up, (me + d) % xs, 1, keepdims=False)
        if d > 0:
            block = lax.ppermute(block, "hidden", [(i, (i + d) % xs) for i in range(xs)])
        gathered = lax.dynamic_update_index_in_dim(gathered, block, (me - d) % xs, 0)
    projected = jnp.sum(exchange(projected, ("ab", "am")).astype(F32), axis=0)
    gate_up = gathered.transpose(2, 1, 0, 3).reshape(chunk, 2 * xs * unit)
    attended = residual[0].astype(F32) + projected
    scale = lax.rsqrt(jnp.mean(attended * attended, axis=1, keepdims=True) + EPSILON)
    normed = (attended * scale * norm_gain).astype(BF16)

    places = lax.axis_size(Z_AXES)
    chosen = expert_ids[0].reshape(2 * owned)
    slots = slot_numbers(chosen, lax.axis_index(Z_AXES), places, capacity).reshape(owned, 2)
    logits = route_logits[0]
    note = note_of(slots, jax.nn.sigmoid(logits[:, 0] - logits[:, 1]))
    noted = jnp.concatenate([normed, note], axis=1)
    tokens = exchange(jnp.broadcast_to(noted, (places, *noted.shape)), Z_AXES)
    tokens = tokens.reshape(places * owned, D + LANES)
    note = tokens[:, D:]

    group_slots = experts * places * capacity
    picked = pick_rows(tokens, group_slots, chunk, parities)
    picked, sent = lax.optimization_barrier((picked, sent))
    other = lax.ppermute(sent, "pair", [(0, 1), (1, 0)])
    rows = exchange(picked.reshape(parities * xs * experts, -1, chunk), ROUTE).reshape(-1, chunk)

    partial = jnp.dot(rows, gate_up, preferred_element_type=F32).astype(BF16)
    partial = partial.reshape(xs, -1, partial.shape[1])
    summed = jnp.sum(exchange(partial, "hidden").astype(F32), axis=0)
    half = xs * unit
    activated = (jax.nn.silu(summed[:, :half]) * summed[:, half:]).astype(BF16)
    activated = exchange(jnp.broadcast_to(activated, (xs, *activated.shape)), "hidden")
    activated = activated.reshape(-1, half)
    kept = kept.reshape(half, width)
    other = other.reshape(half, width)
    down = jnp.concatenate(
        [jnp.where(z_hi == 0, kept, other), jnp.where(z_hi == 0, other, kept)], axis=1
    )
    out = jnp.dot(activated, down, preferred_element_type=F32).astype(BF16)

    returned = exchange(out.reshape(parities * xs * experts, -1, chunk), ROUTE)
    returned = combine_rows(
        note, returned.reshape(parities, xs, group_slots, chunk), owned
    )
    mixed = exchange(returned, Z_AXES)
    layer_out = attended + jnp.sum(mixed.astype(F32), axis=0)
    return layer_out.astype(BF16)[None]


def solution(mesh):
    cut = Mesh(
        mesh.devices.reshape(2, 2, 2, 4, 2, 4, 2),
        ("ab", "am", "al", "y", "core", "hidden", "pair"),
    )
    expert = ("y", "core")
    group = ("y", "core", "pair")
    owner = (*ATTN, "hidden")
    in_specs = (
        P(group, None, owner),
        P(group, None, ATTN),
        P(group, None, ATTN),
        P(owner, None),
        P(group, owner, None),
        P(),
        P(group, owner, None),
        P(group, owner, None),
        P(group, None),
        P(expert, None, None, (*owner, "pair")),
        P(expert, ATTN, ("hidden", "pair")),
    )
    return jax.shard_map(
        layer, mesh=cut, in_specs=in_specs, out_specs=P(group, owner, None), check_vma=False
    )
```

```python
import jax
import jax.numpy as jnp
from jax import lax
from jax.experimental import pallas as pl
from jax.experimental.pallas import tpu as pltpu
from jax.sharding import Mesh
from jax.sharding import PartitionSpec as P


D = 4096
HD = 128
EPSILON = 1e-05
BF16 = jnp.bfloat16
F32 = jnp.float32


ATTN = ("ab", "am", "al")
Z_AXES = ("pair", "ab", "am")
ROUTE = ("al", "hidden", "y", "core")
LANES = 128


def exchange(value, axes):
    return lax.all_to_all(value, axes, 0, 0, tiled=True)


def attention_kernel(doc_ref, queries_ref, keys_ref, values_ref, weight_ref, out_ref):
    count = queries_ref.shape[0]
    first_end = doc_ref[0]
    second_end = first_end + doc_ref[1]
    rows = lax.broadcasted_iota(jnp.int32, (count, count), 0)
    cols = lax.broadcasted_iota(jnp.int32, (count, count), 1)
    row_doc = (rows >= first_end).astype(jnp.int32) + (rows >= second_end).astype(jnp.int32)
    col_doc = (cols >= first_end).astype(jnp.int32) + (cols >= second_end).astype(jnp.int32)
    allowed = (row_doc == col_doc) & (cols <= rows)
    scores = lax.dot_general(
        queries_ref[...],
        keys_ref[...],
        (((1,), (1,)), ((), ())),
        preferred_element_type=F32,
    )
    scores = jnp.where(allowed, scores * HD ** (-0.5), -1e30)
    weights = jnp.exp(scores - jnp.max(scores, axis=1, keepdims=True))
    probabilities = (weights / jnp.sum(weights, axis=1, keepdims=True)).astype(BF16)
    heads_out = jnp.dot(probabilities, values_ref[...], preferred_element_type=F32).astype(BF16)
    total = jnp.dot(heads_out, weight_ref[...], preferred_element_type=F32)
    parts, groups, owned, _ = out_ref.shape
    places = parts // 2
    for group in range(groups):
        for part in range(parts):
            start = ((group * 2 + part // places) * places + part % places) * owned
            out_ref[part, group] = total[start : start + owned].astype(BF16)


def attention(doc_lengths, queries, keys, values, out_weight, parts, owned):
    count = queries.shape[0]
    vmem = pl.BlockSpec(memory_space=pltpu.VMEM)
    return pl.pallas_call(
        attention_kernel,
        in_specs=[pl.BlockSpec(memory_space=pltpu.SMEM), vmem, vmem, vmem, vmem],
        out_specs=vmem,
        out_shape=jax.ShapeDtypeStruct((parts, count // (parts * owned), owned, D), BF16),
        name="attention",
    )(doc_lengths, queries, keys, values, out_weight)


def slot_numbers(chosen, place, places, capacity):
    rows = chosen.shape[0]
    row_ids = jnp.arange(rows, dtype=jnp.int32)
    earlier = row_ids[None, :] < row_ids[:, None]
    same = chosen[:, None] == chosen[None, :]
    ranking = jnp.sum((same & earlier).astype(jnp.int32), axis=-1)
    return (chosen * places + place) * capacity + ranking


def note_of(slots, share):
    high = lax.reduce_precision(share, 8, 7)
    middle = lax.reduce_precision(share - high, 8, 7)
    low = share - high - middle
    parts = jnp.stack([slots[:, 0].astype(F32), slots[:, 1].astype(F32), high, middle, low], axis=1)
    return jnp.pad(parts, ((0, 0), (0, LANES - 5))).astype(BF16)


def stacked(ref):
    return jnp.concatenate([ref[k].astype(F32) for k in range(ref.shape[0])], axis=0)


def pick_kernel(tokens_ref, note_ref, out_ref):
    note = stacked(note_ref)
    slots = lax.broadcasted_iota(jnp.int32, (note.shape[0], out_ref.shape[2]), 1).astype(F32)
    taken = (slots == note[:, 0:1]) | (slots == note[:, 1:2])
    rows = lax.dot_general(
        jnp.where(taken, 1.0, 0.0).astype(BF16),
        stacked(tokens_ref).astype(BF16),
        (((0,), (0,)), ((), ())),
        preferred_element_type=F32,
    ).astype(BF16)
    for copy in range(out_ref.shape[0]):
        out_ref[copy, 0] = rows


def pick_rows(tokens, slots, chunk, copies):
    places, owned, _ = tokens.shape
    return pl.pallas_call(
        pick_kernel,
        grid=(D // chunk,),
        in_specs=[
            pl.BlockSpec((places, owned, chunk), lambda j: (0, 0, j)),
            pl.BlockSpec((places, owned, LANES), lambda j: (0, 0, D // LANES)),
        ],
        out_specs=pl.BlockSpec((copies, 1, slots, chunk), lambda j: (0, j, 0, 0)),
        out_shape=jax.ShapeDtypeStruct((copies, D // chunk, slots, chunk), BF16),
        name="pick",
    )(tokens, tokens)


def combine_kernel(note_ref, rows_ref, out_ref):
    note = stacked(note_ref)
    share = note[:, 2:3] + note[:, 3:4] + note[:, 4:5]
    slots = lax.broadcasted_iota(jnp.int32, (note.shape[0], rows_ref.shape[2]), 1).astype(F32)
    weight = jnp.where(slots == note[:, 0:1], share, 0.0)
    weight = weight + jnp.where(slots == note[:, 1:2], 1.0 - share, 0.0)
    high = weight.astype(BF16)
    low = (weight - high.astype(F32)).astype(BF16)
    both = jnp.concatenate([high, low], axis=0)
    total = jnp.zeros((2 * note.shape[0], out_ref.shape[2]), F32)
    for k in range(rows_ref.shape[0]):
        total += jnp.dot(both, rows_ref[k, 0], preferred_element_type=F32)
    total = total[: note.shape[0]] + total[note.shape[0] :]
    places, owned, _ = out_ref.shape
    for place in range(places):
        out_ref[place] = total[place * owned : (place + 1) * owned].astype(BF16)


def combine_rows(tokens, rows):
    places, owned, _ = tokens.shape
    sums, chunks, slots, chunk = rows.shape
    return pl.pallas_call(
        combine_kernel,
        grid=(chunks,),
        in_specs=[
            pl.BlockSpec((places, owned, LANES), lambda j: (0, 0, D // LANES)),
            pl.BlockSpec((sums, 1, slots, chunk), lambda j: (0, j, 0, 0)),
        ],
        out_specs=pl.BlockSpec((places, owned, chunk), lambda j: (0, 0, j)),
        out_shape=jax.ShapeDtypeStruct((places, owned, chunks * chunk), BF16),
        name="combine",
    )(tokens, rows)


def layer(
    queries,
    keys,
    values,
    out_weight,
    residual,
    norm_gain,
    route_logits,
    expert_ids,
    doc_lengths,
    gate_up_weight,
    down_weight,
):
    xs = lax.axis_size("hidden")
    zl = lax.axis_size(ATTN)
    parities = lax.axis_size("al")
    pairs = lax.axis_size("pair")
    experts = lax.axis_size(("y", "core"))
    capacity = 2
    chunk = D // xs
    z_hi = lax.axis_index("pair")

    unit = gate_up_weight.shape[-1]
    down = down_weight[0].reshape(xs, pairs, unit, -1)
    width = down.shape[-1]
    kept = lax.dynamic_index_in_dim(down, z_hi, 1, keepdims=False)
    sent = lax.dynamic_index_in_dim(down, 1 - z_hi, 1, keepdims=False)

    tok_group = queries.shape[1]
    owned = tok_group // (zl * xs)
    projected = attention(
        doc_lengths[0], queries[0], keys[0], values[0], out_weight, parities * xs, owned
    )
    projected = exchange(projected, ("al", "hidden"))
    projected = jnp.sum(projected.astype(F32), axis=0).astype(BF16)
    gate_up = gate_up_weight[0].reshape(2, xs, chunk, unit)
    me = lax.axis_index("hidden")
    gathered = jnp.zeros((xs, 2, chunk, unit), BF16)
    for d in range(xs):
        block = lax.dynamic_index_in_dim(gate_up, (me + d) % xs, 1, keepdims=False)
        if d > 0:
            block = lax.ppermute(block, "hidden", [(i, (i + d) % xs) for i in range(xs)])
        gathered = lax.dynamic_update_index_in_dim(gathered, block, (me - d) % xs, 0)
    projected = jnp.sum(exchange(projected, ("ab", "am")).astype(F32), axis=0)
    gate_up = gathered.transpose(2, 1, 0, 3).reshape(chunk, 2 * xs * unit)
    attended = residual[0].astype(F32) + projected
    scale = lax.rsqrt(jnp.mean(attended * attended, axis=1, keepdims=True) + EPSILON)
    normed = (attended * scale * norm_gain).astype(BF16)

    places = lax.axis_size(Z_AXES)
    chosen = expert_ids[0].reshape(2 * owned)
    slots = slot_numbers(chosen, lax.axis_index(Z_AXES), places, capacity).reshape(owned, 2)
    logits = route_logits[0]
    note = note_of(slots, jax.nn.sigmoid(logits[:, 0] - logits[:, 1]))
    noted = jnp.concatenate([normed, note], axis=1)
    tokens = exchange(jnp.broadcast_to(noted, (places, *noted.shape)), Z_AXES)

    group_slots = experts * places * capacity
    picked = pick_rows(tokens, group_slots, chunk, parities)
    picked, sent = lax.optimization_barrier((picked, sent))
    other = lax.ppermute(sent, "pair", [(0, 1), (1, 0)])
    rows = exchange(picked.reshape(parities * xs * experts, -1, chunk), ROUTE).reshape(-1, chunk)

    partial = jnp.dot(rows, gate_up, preferred_element_type=F32).astype(BF16)
    partial = partial.reshape(xs, -1, partial.shape[1])
    summed = jnp.sum(exchange(partial, "hidden").astype(F32), axis=0)
    half = xs * unit
    activated = (jax.nn.silu(summed[:, :half]) * summed[:, half:]).astype(BF16)
    activated = exchange(jnp.broadcast_to(activated, (xs, *activated.shape)), "hidden")
    activated = activated.reshape(-1, half)
    kept = kept.reshape(half, width)
    other = other.reshape(half, width)
    down = jnp.concatenate(
        [jnp.where(z_hi == 0, kept, other), jnp.where(z_hi == 0, other, kept)], axis=1
    )
    out = jnp.dot(activated, down, preferred_element_type=F32).astype(BF16)

    returned = exchange(out.reshape(parities * xs * experts, -1, chunk), ROUTE)
    returned = combine_rows(tokens, returned.reshape(parities, xs, group_slots, chunk))
    mixed = exchange(returned, Z_AXES)
    layer_out = attended + jnp.sum(mixed.astype(F32), axis=0)
    return layer_out.astype(BF16)[None]


def solution(mesh):
    cut = Mesh(
        mesh.devices.reshape(2, 2, 2, 4, 2, 4, 2),
        ("ab", "am", "al", "y", "core", "hidden", "pair"),
    )
    expert = ("y", "core")
    group = ("y", "core", "pair")
    owner = (*ATTN, "hidden")
    in_specs = (
        P(group, None, owner),
        P(group, None, ATTN),
        P(group, None, ATTN),
        P(owner, None),
        P(group, owner, None),
        P(),
        P(group, owner, None),
        P(group, owner, None),
        P(group, None),
        P(expert, None, None, (*owner, "pair")),
        P(expert, ATTN, ("hidden", "pair")),
    )
    return jax.shard_map(
        layer, mesh=cut, in_specs=in_specs, out_specs=P(group, owner, None), check_vma=False
    )
```
